32 devices in a mesh: groups: 2 (over y), sect: 16 (over z, x, core).
Axes of the slice: x: 2, y: 2, z: 4, core: 2. Of those that a mesh axis runs over, the one named last changes fastest.
Arguments:
- pattern: int32 [32], P('sect'), may hold values from 0 to 15
- thickness: float32 [32], P('sect'), may hold values from 0.5 to 1.5
- coupling: float32 [16, 2, 169, 169], replicated, may hold values from -0.0625 to 0.0625
- angles: float32 [64, 169], replicated, may hold values from -3.140625 to 3.140625
- points: int32 [2], P('groups'), parts along dimension 0, may hold values from 0 to 63
- incident: float32 [2, 2, 169, 169], P('groups'), parts along dimension 0, may hold values from -6 to 6
- monitors: int32 [16], replicated, may hold values from 0 to 168
- weights: float32 [16], replicated, may hold values from 0.05 to 0.5
Outputs:
- fields: float32 [32, 2, 2, 169, 169], P('sect', 'groups'), parts along dimension 1
- gradient: float32 [2, 32], P('groups', 'sect'), parts along dimension 0
The draws below stay inside these ranges and needn't reach their ends.
There are 2 independent parts, one for each index of `groups`. The reference program is written for one: setup_inputs(seed, part) draws one part's arguments, and reference() takes and returns one part's arrays. A program takes and returns all parts, laid end to end along the dimension named above; an argument that names none is the same for every part. Nothing has to cross between parts.
All inputs are finite; a program needn't handle non-finite values.
Results may differ from the reference program's by a relative error of at most 0.0003.
Values sent between devices are 32-bit elements; how exact they have to be, the bound alone decides.
A program may use at most 128 MiB of HBM per device.

```python
import math
import jax
import jax.numpy as jnp
from jax import lax

HARM = 169
NPAT = 16
NQ = 64
MON = 16
PTS = 1
LAYERS = 32


def place_ends(entries, key, smallest, top_value):
    longest = entries.shape.index(max(entries.shape))
    spots = []
    for shift in (0, 1):
        where = [jax.random.randint(jax.random.fold_in(key, axis), (), 0, length) for axis, length in enumerate(entries.shape)]
        where[longest] = (where[longest] + shift) % entries.shape[longest]
        spots.append(tuple(where))
    return entries.at[spots[0]].set(smallest).at[spots[1]].set(top_value)


def steps_of(own_key, shape, split, smallest, high):
    def one(dim, shards_of):
        heights = jax.random.uniform(jax.random.fold_in(jax.random.fold_in(own_key, 6), dim), (shards_of,), jnp.float32, smallest / len(split), high / len(split))
        return jnp.repeat(jnp.exp(heights), shape[dim] // shards_of).reshape((-1,) + (1,) * (len(shape) - dim - 1))

    factor_of = one(*split[0])
    for cut in split[1:]:
        factor_of = factor_of * one(*cut)
    return factor_of


def bell_draw(stream_key, dims, scale, limit, held_as=jnp.bfloat16):
    values = jax.random.normal(stream_key, dims, jnp.float32) * scale
    return jnp.minimum(jnp.maximum(values, -limit), limit).astype(held_as)


def setup_inputs(seed: int = 0, part: int = 0) -> dict:
    key_list = jax.random.split(jax.random.key(seed), 9)
    part_keys = jax.random.split(jax.random.fold_in(key_list[8], part), 9)
    pattern = place_ends(jax.random.randint(key_list[0], (LAYERS,), 0, NPAT), jax.random.fold_in(key_list[0], 1), 0, NPAT - 1).astype(jnp.int32)
    thickness = jnp.clip(jnp.exp(math.log(1.5) - 1.0986123 * jax.random.uniform(key_list[1], (LAYERS,), jnp.float32) ** steps_of(key_list[1], (LAYERS,), ((0, 16),), -0.2, 0.2)), 0.5, 1.5)
    coupling = bell_draw(key_list[2], (NPAT, 2, HARM, HARM), (44 * HARM) ** -0.5, 0.0625, jnp.float32)
    angles = jnp.clip(jax.random.uniform(key_list[3], (NQ, HARM), jnp.float32, -3.140625, 3.140625), -3.140625, 3.140625)
    points = jax.random.randint(part_keys[4], (PTS,), 0, NQ).astype(jnp.int32)
    incident = bell_draw(part_keys[5], (PTS, 2, HARM, HARM), 1.0, 6.0, jnp.float32)
    monitors = place_ends(jax.random.randint(key_list[6], (MON,), 0, HARM), jax.random.fold_in(key_list[6], 1), 0, HARM - 1).astype(jnp.int32)
    weights = jnp.clip(jnp.exp(jax.random.uniform(key_list[7], (MON,), jnp.float32, math.log(0.05), math.log(0.5))), 0.05, 0.5)
    return {"pattern": pattern, "thickness": thickness, "coupling": coupling, "angles": angles, "points": points, "incident": incident, "monitors": monitors, "weights": weights}


norm_scale = (1.0 + 1.0 / 22.0) ** -0.5
highest = lax.Precision.HIGHEST


def reference(pattern, thickness, coupling, angles, points, incident, monitors, weights):
    angle_rows = angles[points]
    point_count = incident.shape[0]
    identity_matrix = jnp.eye(HARM, dtype=jnp.float32)

    def forward(carried, inputs):
        pattern_id, layer_depth = inputs
        mixing_real = norm_scale * (identity_matrix + coupling[pattern_id, 0])
        mixing_imag = norm_scale * coupling[pattern_id, 1]
        field_real = carried[:, 0]
        field_imag = carried[:, 1]
        mixed_real = jnp.einsum("ij,pjk->pik", mixing_real, field_real, precision=highest) - jnp.einsum("ij,pjk->pik", mixing_imag, field_imag, precision=highest)
        mixed_imag = jnp.einsum("ij,pjk->pik", mixing_imag, field_real, precision=highest) + jnp.einsum("ij,pjk->pik", mixing_real, field_imag, precision=highest)
        cosine = jnp.cos(angle_rows * layer_depth)[:, :, None]
        sine_part = jnp.sin(angle_rows * layer_depth)[:, :, None]
        updated = jnp.stack([cosine * mixed_real - sine_part * mixed_imag, cosine * mixed_imag + sine_part * mixed_real], axis=1)
        return updated, updated

    last_field, fields = lax.scan(forward, incident, (pattern, thickness))
    selector = jnp.sum(jnp.where(monitors[:, None] == jnp.arange(HARM)[None, :], weights[:, None], 0.0), axis=0)
    adjoint = last_field * selector[None, None, :, None] / (point_count * HARM)

    def backward(carried, inputs):
        pattern_id, layer_depth, layer_field = inputs
        adj_real = carried[:, 0]
        adj_imag = carried[:, 1]
        contribution = -2.0 * jnp.sum(angle_rows[:, :, None] * (adj_real * layer_field[:, 1] - adj_imag * layer_field[:, 0]))
        cosine = jnp.cos(angle_rows * layer_depth)[:, :, None]
        sine_part = jnp.sin(angle_rows * layer_depth)[:, :, None]
        back_real = cosine * adj_real + sine_part * adj_imag
        back_imag = cosine * adj_imag - sine_part * adj_real
        mixing_real = norm_scale * (identity_matrix + coupling[pattern_id, 0])
        mixing_imag = norm_scale * coupling[pattern_id, 1]
        new_real = jnp.einsum("ji,pjk->pik", mixing_real, back_real, precision=highest) + jnp.einsum("ji,pjk->pik", mixing_imag, back_imag, precision=highest)
        new_imag = jnp.einsum("ji,pjk->pik", mixing_real, back_imag, precision=highest) - jnp.einsum("ji,pjk->pik", mixing_imag, back_real, precision=highest)
        return jnp.stack([new_real, new_imag], axis=1), contribution

    unused, gradient = lax.scan(backward, adjoint, (pattern, thickness, fields), reverse=True)
    return fields, gradient[None, :]
```

```python
import functools
import jax
import jax.numpy as jnp
from jax import lax
from jax.experimental import pallas as pl
from jax.experimental.pallas import tpu as pltpu
from jax.sharding import PartitionSpec as P

norm_scale = (1.0 + 1.0 / 22.0) ** (-0.5)
f32 = jnp.float32
bf16 = jnp.bfloat16
LANES = 128


def cut_of(harm):
    cut = harm // LANES * LANES
    rest = harm - cut
    assert 3 * rest <= LANES
    return cut, rest


def split(x):
    hi = x.astype(bf16)
    return hi, (x - hi.astype(f32)).astype(bf16)


def depth_of(harm):
    return 3 * cut_of(harm)[0] + LANES


def left(x):
    cut, rest = cut_of(x.shape[1])
    hi, lo = split(x)
    a, b = hi[:, cut:], lo[:, cut:]
    zero = jnp.zeros((x.shape[0], LANES - 3 * rest), bf16)
    return jnp.concatenate([hi[:, :cut], lo[:, :cut], hi[:, :cut], a, b, a, zero], axis=1)


def right_parts(x):
    cut, rest = cut_of(x.shape[0])
    hi = x.astype(bf16)
    wide = hi.astype(f32)
    lo = x - wide
    zero = jnp.zeros((LANES - 3 * rest, x.shape[1]), f32)
    tail = jnp.concatenate([wide[cut:], wide[cut:], lo[cut:], zero], axis=0)
    return hi[:cut], lo[:cut].astype(bf16), tail.astype(bf16)


def right(x):
    hi, lo, tail = right_parts(x)
    return jnp.concatenate([hi, hi, lo, tail], axis=0)


def rights(real, imag):
    return [right(real), right(imag - real), right(real + imag)]


def dot(a, b):
    return lax.dot_general(a, b, (((1,), (0,)), ((), ())), preferred_element_type=f32)


def product(real, imag, weights):
    both = dot(left(real + imag), weights[0])
    first = dot(left(real), weights[1])
    second = dot(left(imag), weights[2])
    return both - second, both + first


def store_right(ref, at, x):
    hi, lo, tail = right_parts(x)
    cut = hi.shape[0]
    ref[at + (pl.ds(0, cut),)] = hi
    ref[at + (pl.ds(cut, cut),)] = hi
    ref[at + (pl.ds(2 * cut, cut),)] = lo
    ref[at + (pl.ds(3 * cut, LANES),)] = tail


def gather_kernel(
    count, pattern, thickness, coupling, incident,
    out_ref, mixing, weights, start, own_ref, waves, send_sem, recv_sem, load_sem, wave_sem,
):
    here = lax.axis_index("sect")
    barrier = pltpu.get_barrier_semaphore()
    patterns = coupling.shape[0]
    harm = coupling.shape[-1]

    def peer(k):
        return lax.rem(here + k, count)

    for k in range(1, count):
        pl.semaphore_signal(barrier, inc=1, device_id={"sect": peer(k)}, device_id_type=pl.DeviceIdType.MESH)

    def load(n, r):
        return pltpu.make_async_copy(coupling.at[n, :, r, :], mixing.at[n, r], load_sem.at[n, r])

    def load_start(n, c):
        load(n, 0).start()
        load(n, 1).start()
        return c

    lax.fori_loop(0, patterns, load_start, 0)
    wave = [
        pltpu.make_async_copy(incident.at[0, :, r, :], waves.at[r], wave_sem.at[r]) for r in range(2)
    ]
    for copy in wave:
        copy.start()

    lanes = lax.broadcasted_iota(jnp.int32, (1, LANES), 1)
    own = jnp.zeros((1, LANES), f32)
    own_layers = pattern.shape[0]
    for j in range(own_layers):
        own = jnp.where(lanes == j, pattern[j].astype(f32), own)
        own = jnp.where(lanes == own_layers + j, thickness[j], own)
    own_ref[...] = own
    out_ref[here] = own
    pl.semaphore_wait(barrier, count - 1)

    copies = [
        pltpu.make_async_remote_copy(
            src_ref=own_ref,
            dst_ref=out_ref.at[here],
            send_sem=send_sem.at[k],
            recv_sem=recv_sem.at[k],
            device_id={"sect": peer(k)},
            device_id_type=pl.DeviceIdType.MESH,
        )
        for k in range(1, count)
    ]
    for copy in copies:
        copy.start()

    rows = lax.broadcasted_iota(jnp.int32, (harm, harm), 0)
    columns = lax.broadcasted_iota(jnp.int32, (harm, harm), 1)
    unit = jnp.where(rows == columns, 1.0, 0.0).astype(f32)

    def prepare(n, c):
        load(n, 0).wait()
        load(n, 1).wait()
        real, imag = unit + mixing[n, 0], mixing[n, 1]
        store_right(weights, (n, 0), real)
        store_right(weights, (n, 1), imag - real)
        store_right(weights, (n, 2), real + imag)
        return c

    lax.fori_loop(0, patterns, prepare, 0)
    for copy in wave:
        copy.wait()
    real, imag = waves[0], waves[1]
    store_right(start, (0,), real)
    store_right(start, (1,), imag - real)
    store_right(start, (2,), real + imag)
    for copy in copies:
        copy.wait()


def main_kernel(
    sections, own_layers, gathered, points, monitors, strengths, mixing, weights, start, angles,
    fields, gradient, cosines, sines, kept, out_sem,
):
    here = lax.axis_index("sect")
    layers = sections * own_layers
    harm = angles.shape[-1]
    mon = monitors.shape[0]
    first = here * own_layers
    last = first + 1

    def pattern_of(layer):
        return gathered[layer // own_layers, 0, lax.rem(layer, own_layers)].astype(jnp.int32)

    theta = angles[pl.ds(points[0], 1), :]

    def fill(layer, c):
        depth = gathered[layer // own_layers, 0, own_layers + lax.rem(layer, own_layers)]
        cosines[pl.ds(layer, 1), :] = theta * depth
        return c

    lax.fori_loop(0, layers, fill, 0, unroll=8)
    turn = cosines[...]
    sines[...] = norm_scale * jnp.sin(turn)
    cosines[...] = norm_scale * jnp.cos(turn)

    rows = lax.broadcasted_iota(jnp.int32, (harm, harm), 0)
    columns = lax.broadcasted_iota(jnp.int32, (harm, harm), 1)
    unit = jnp.where(rows == columns, 1.0, 0.0).astype(f32)
    none = jnp.zeros((harm, harm), f32)

    def transfer(layer):
        n = pattern_of(layer)
        cos = jnp.broadcast_to(cosines[pl.ds(layer, 1), :], (8, harm)).T[:, 0:1]
        sin = jnp.broadcast_to(sines[pl.ds(layer, 1), :], (8, harm)).T[:, 0:1]
        real, imag = unit + mixing[n, 0], mixing[n, 1]
        return cos * real - sin * imag, cos * imag + sin * real

    def step(layer, real, imag):
        cos, sin = cosines[pl.ds(layer, 1), :], sines[pl.ds(layer, 1), :]
        n = pattern_of(layer)
        return product(
            cos * real - sin * imag, cos * imag + sin * real,
            (weights[n, 0], weights[n, 1], weights[n, 2]),
        )

    def pairs(count, one, two, state):
        def body(i, c):
            return step(one - i, c[0], c[1]) + step(two - i, c[2], c[3])

        def three(i, c):
            for j in range(3):
                c = body(3 * i + j, c)
            return c

        state = lax.fori_loop(0, count // 3, three, state)
        return lax.fori_loop(count // 3 * 3, count, body, state)

    pick_rows = lax.broadcasted_iota(jnp.int32, (mon, harm), 0)
    pick_lanes = lax.broadcasted_iota(jnp.int32, (mon, harm), 1)
    picked = jnp.zeros((mon, harm), f32)
    scale = jnp.zeros((mon, harm), f32)
    for m in range(mon):
        picked = jnp.where((pick_rows == m) & (pick_lanes == monitors[m]), 1.0, picked)
        scale = jnp.where(pick_rows == m, strengths[m], scale)
    scale = scale * (1.0 / harm)

    half = (layers - first - own_layers) // 2
    row_real, row_imag, real, imag = pairs(
        half, layers - 1, layers - 1 - half, (picked, jnp.zeros_like(picked), unit, none)
    )
    row_real, row_imag = product(row_real, row_imag, rights(real, imag))
    two_real = jnp.concatenate([row_real, row_real * theta], axis=0)
    two_imag = jnp.concatenate([row_imag, row_imag * theta], axis=0)
    two_real, two_imag = step(last, two_real, two_imag)
    last_real, last_imag = transfer(last)
    gap = jnp.zeros((-harm % 16, harm), f32)
    full_real = jnp.concatenate([last_real, gap, two_real[:mon] * theta, two_real], axis=0)
    full_imag = jnp.concatenate([last_imag, gap, two_imag[:mon] * theta, two_imag], axis=0)

    half = first // 2
    real, imag = transfer(first)
    top_real, top_imag, real, imag = pairs(half, first - 1, half - 1, (real, imag, unit, none))
    real, imag = product(real, imag, (start[0], start[1], start[2]))
    real, imag = product(top_real, top_imag, rights(real, imag))
    kept[0, 0], kept[0, 1] = real, imag

    def out(j, r):
        return pltpu.make_async_copy(kept.at[j, r], fields.at[j, 0, :, r, :], out_sem.at[j, r])

    out(0, 0).start()
    out(0, 1).start()
    real, imag = product(full_real, full_imag, rights(real, imag))
    kept[1, 0], kept[1, 1] = real[:harm], imag[:harm]
    out(1, 0).start()
    out(1, 1).start()
    at = harm + gap.shape[0]
    seen_real, seen_imag = real[at + mon : at + 2 * mon] * scale, imag[at + mon : at + 2 * mon] * scale
    for j, top in enumerate((at, at + 2 * mon)):
        total = jnp.sum(seen_real * imag[top : top + mon] - seen_imag * real[top : top + mon])
        gradient[0, j] = -2.0 * total
    for j in range(2):
        out(j, 0).wait()
        out(j, 1).wait()


def local(pattern, thickness, coupling, angles, points, incident, monitors, weights):
    sections = lax.axis_size("sect")
    own_layers = pattern.shape[0]
    assert own_layers == 2
    patterns, harm = coupling.shape[0], incident.shape[-1]
    layers = sections * own_layers
    depth = depth_of(harm)
    vmem = pl.BlockSpec(memory_space=pltpu.VMEM)
    smem = pl.BlockSpec(memory_space=pltpu.SMEM)
    hbm = pl.BlockSpec(memory_space=pltpu.HBM)
    gathered, mixing, prepared, start = pl.pallas_call(
        functools.partial(gather_kernel, sections),
        out_shape=(
            jax.ShapeDtypeStruct((sections, 1, LANES), f32),
            jax.ShapeDtypeStruct((patterns, 2, harm, harm), f32),
            jax.ShapeDtypeStruct((patterns, 3, depth, harm), bf16),
            jax.ShapeDtypeStruct((3, depth, harm), bf16),
        ),
        in_specs=[smem, smem, hbm, hbm],
        out_specs=(vmem, vmem, vmem, vmem),
        scratch_shapes=[
            pltpu.VMEM((1, LANES), f32),
            pltpu.VMEM((2, harm, harm), f32),
            pltpu.SemaphoreType.DMA((sections,)),
            pltpu.SemaphoreType.DMA((sections,)),
            pltpu.SemaphoreType.DMA((patterns, 2)),
            pltpu.SemaphoreType.DMA((2,)),
        ],
        compiler_params=pltpu.CompilerParams(
            collective_id=0, has_side_effects=True, vmem_limit_bytes=4 * 2**20
        ),
    )(
        pattern,
        thickness,
        pltpu.with_memory_space_constraint(coupling.transpose(0, 2, 1, 3), pltpu.HBM),
        pltpu.with_memory_space_constraint(incident.transpose(0, 2, 1, 3), pltpu.HBM),
    )
    fields, gradient = pl.pallas_call(
        functools.partial(main_kernel, sections, own_layers),
        out_shape=(
            jax.ShapeDtypeStruct((own_layers, 1, harm, 2, harm), f32),
            jax.ShapeDtypeStruct((1, own_layers), f32),
        ),
        in_specs=[smem, smem, smem, smem, vmem, vmem, vmem, vmem],
        out_specs=(hbm, smem),
        scratch_shapes=[
            pltpu.VMEM((layers, harm), f32),
            pltpu.VMEM((layers, harm), f32),
            pltpu.VMEM((2, 2, harm, harm), f32),
            pltpu.SemaphoreType.DMA((2, 2)),
        ],
        compiler_params=pltpu.CompilerParams(vmem_limit_bytes=16 * 2**20),
    )(gathered, points, monitors, weights, mixing, prepared, start, angles)
    return fields.transpose(0, 1, 3, 2, 4), gradient


def solution(mesh):
    in_specs = (
        P("sect"), P("sect"), P(), P(), P("groups"),
        P("groups", None, None, None), P(), P(),
    )
    out_specs = (P("sect", "groups", None, None, None), P("groups", "sect"))
    return jax.shard_map(local, mesh=mesh, in_specs=in_specs, out_specs=out_specs, check_vma=False)
```

```python
import functools
import math
import jax
import jax.numpy as jnp
from jax import lax
from jax.experimental import pallas as pl
from jax.experimental.pallas import tpu as pltpu
from jax.sharding import PartitionSpec as P

norm_scale = (1.0 + 1.0 / 22.0) ** (-0.5)
f32 = jnp.float32
bf16 = jnp.bfloat16
LANES = 128
UNROLL = (5, 2, 1)


def cut_of(harm):
    cut = harm // LANES * LANES
    rest = harm - cut
    assert 3 * rest <= LANES
    return cut, rest


def split(x):
    hi = x.astype(bf16)
    return hi, (x - hi.astype(f32)).astype(bf16)


def depth_of(harm):
    return 3 * cut_of(harm)[0] + LANES


def left(x):
    cut, rest = cut_of(x.shape[1])
    hi, lo = split(x)
    a, b = hi[:, cut:], lo[:, cut:]
    zero = jnp.zeros((x.shape[0], LANES - 3 * rest), bf16)
    return jnp.concatenate([hi[:, :cut], lo[:, :cut], hi[:, :cut], a, b, a, zero], axis=1)


def right_parts(x):
    cut, rest = cut_of(x.shape[0])
    hi = x.astype(bf16)
    wide = hi.astype(f32)
    lo = x - wide
    zero = jnp.zeros((LANES - 3 * rest, x.shape[1]), f32)
    tail = jnp.concatenate([wide[cut:], wide[cut:], lo[cut:], zero], axis=0)
    return hi[:cut], lo[:cut].astype(bf16), tail.astype(bf16)


def right(x):
    hi, lo, tail = right_parts(x)
    return jnp.concatenate([hi, hi, lo, tail], axis=0)


def rights(real, imag):
    return [right(real), right(imag - real), right(real + imag)]


def dot(a, b):
    return lax.dot_general(a, b, (((1,), (0,)), ((), ())), preferred_element_type=f32)


def lefts(real, imag):
    return left(real + imag), left(real), left(imag)


def multiply(operands, weights):
    both, first, second = (dot(x, y) for x, y in zip(operands, weights))
    return both - second, both + first


def product(real, imag, weights):
    return multiply(lefts(real, imag), weights)


def product_rows(real, imag, weights):
    m = real.shape[0]
    both = left(jnp.concatenate([real + imag, real - imag], axis=0))
    low, high = dot(both, weights[1]), dot(both, weights[2])
    return 0.5 * (high[m:] - low[:m]), 0.5 * (high[:m] + low[m:])


def turns_of(x):
    k = jnp.floor(x * (2.0 / math.pi) + 0.5)
    r = ((x - k * 1.5703125) - k * 4.837512969970703e-4) - k * 7.549789948768648e-8
    z = r * r
    sin = r + r * z * (-1.6666654611e-1 + z * (8.3321608736e-3 + z * -1.9515295891e-4))
    cos = 1.0 - 0.5 * z + z * z * (
        4.166664568298827e-2 + z * (-1.388731625493765e-3 + z * 2.443315711809948e-5)
    )
    q = k.astype(jnp.int32) & 3
    odd = (q & 1) == 1
    cos, sin = jnp.where(odd, sin, cos), jnp.where(odd, cos, sin)
    cos = jnp.where((q == 1) | (q == 2), -cos, cos)
    sin = jnp.where(q >= 2, -sin, sin)
    return norm_scale * cos, norm_scale * sin


def store_right(ref, at, x):
    hi, lo, tail = right_parts(x)
    cut = hi.shape[0]
    ref[at + (pl.ds(0, cut),)] = hi
    ref[at + (pl.ds(cut, cut),)] = hi
    ref[at + (pl.ds(2 * cut, cut),)] = lo
    ref[at + (pl.ds(3 * cut, LANES),)] = tail


def each(low, high, act):
    if high - low <= 16:
        for k in range(low, high):
            act(k)
    else:
        lax.fori_loop(low, high, lambda k, c: (act(k), c)[1], 0)


def gather_kernel(
    count, pattern, thickness, angles, monitors, strengths, coupling, incident, points,
    out_ref, index_ref, theta_ref, picked_ref, scale_ref, head, tail, weights, start,
    own_pattern, own_thickness, own_angles, own_monitors, own_strengths, own_ref, waves, mixing,
    own_sem, send_sem, recv_sem, load_sem, wave_sem,
):
    here = lax.axis_index("sect")
    barrier = pltpu.get_barrier_semaphore()
    patterns = coupling.shape[0]
    harm = coupling.shape[-1]
    own_layers = pattern.shape[0]
    mesh_id = pl.DeviceIdType.MESH

    def peer(k):
        return lax.rem(here + k, count)

    def greet(k):
        pl.semaphore_signal(barrier, inc=1, device_id={"sect": peer(k)}, device_id_type=mesh_id)

    own_copies = [
        pltpu.make_async_copy(source, target, own_sem.at[k])
        for k, (source, target) in enumerate((
            (pattern, own_pattern), (thickness, own_thickness), (angles, own_angles),
            (monitors, own_monitors), (strengths, own_strengths),
        ))
    ]
    for copy in own_copies:
        copy.start()
    each(1, count, greet)

    bunch = 4 if patterns % 4 == 0 else 1
    bunches = patterns // bunch

    def load(b, r):
        some = pl.ds(b * bunch, bunch)
        return pltpu.make_async_copy(coupling.at[some, :, r, :], mixing.at[some, r], load_sem.at[b, r])

    def load_start(b, c):
        load(b, 0).start()
        load(b, 1).start()
        return c

    lax.fori_loop(0, bunches, load_start, 0)
    wave = [
        pltpu.make_async_copy(incident.at[0, :, r, :], waves.at[r], wave_sem.at[r]) for r in range(2)
    ]
    for copy in wave:
        copy.start()

    for copy in own_copies[:2]:
        copy.wait()
    lanes = lax.broadcasted_iota(jnp.int32, (1, LANES), 1)
    own = jnp.zeros((1, LANES), f32)
    for j in range(own_layers):
        own = jnp.where(lanes == j, own_pattern[j].astype(f32), own)
        own = jnp.where(lanes == own_layers + j, own_thickness[j], own)
    own_ref[...] = own
    out_ref[here] = own
    rows = lax.broadcasted_iota(jnp.int32, (harm, harm), 0)
    columns = lax.broadcasted_iota(jnp.int32, (harm, harm), 1)
    unit = jnp.where(rows == columns, 1.0, 0.0).astype(f32)

    def prepare_one(n, c):
        real, imag = unit + mixing[n, 0], mixing[n, 1]
        store_right(weights, (n, 0), real)
        store_right(weights, (n, 1), imag - real)
        store_right(weights, (n, 2), real + imag)
        return c

    def prepare(b, c):
        load(b, 0).wait()
        load(b, 1).wait()
        return lax.fori_loop(b * bunch, (b + 1) * bunch, prepare_one, c)

    early = jnp.where(here < 2, bunches // 2, jnp.where(here < count // 2, bunches // 4, 0))
    lax.fori_loop(0, early, prepare, 0)
    pl.semaphore_wait(barrier, count - 1)

    def send(k):
        return pltpu.make_async_remote_copy(
            src_ref=own_ref,
            dst_ref=out_ref.at[here],
            send_sem=send_sem.at[k],
            recv_sem=recv_sem.at[k],
            device_id={"sect": peer(k)},
            device_id_type=mesh_id,
        )

    each(1, count, lambda k: send(k).start())

    for copy in own_copies[2:]:
        copy.wait()
    entries = lax.broadcasted_iota(jnp.int32, own_angles.shape, 0)
    theta = jnp.sum(jnp.where(entries == points[...], own_angles[...], 0.0), axis=0, keepdims=True)
    theta_ref[...] = theta
    mon = monitors.shape[0]
    pick_rows = lax.broadcasted_iota(jnp.int32, (mon, harm), 0)
    pick_lanes = lax.broadcasted_iota(jnp.int32, (mon, harm), 1)
    picked = jnp.zeros((mon, harm), f32)
    scale = jnp.zeros((mon, harm), f32)
    for m in range(mon):
        picked = jnp.where((pick_rows == m) & (pick_lanes == own_monitors[m]), 1.0, picked)
        scale = jnp.where(pick_rows == m, own_strengths[m], scale)
    picked_ref[...] = picked
    scale_ref[...] = scale * (1.0 / harm)
    turns = jnp.concatenate([theta * own_thickness[j] for j in range(own_layers)], axis=0)
    turns = jnp.concatenate([*turns_of(turns), jnp.zeros((8 - 2 * own_layers, harm), f32)], axis=0).T

    lax.fori_loop(early, bunches, prepare, 0)
    for copy in wave:
        copy.wait()
    real, imag = waves[0], waves[1]
    store_right(start, (0,), real)
    store_right(start, (1,), imag - real)
    store_right(start, (2,), real + imag)

    def transfer(j):
        cos, sin = turns[:, j : j + 1], turns[:, own_layers + j : own_layers + j + 1]
        n = own_pattern[j]
        real, imag = unit + mixing[n, 0], mixing[n, 1]
        return cos * real - sin * imag, cos * imag + sin * real

    head[0], head[1] = transfer(0)
    gap = jnp.zeros((-harm % 16, harm), f32)
    real, imag = (jnp.concatenate([x, gap], axis=0) for x in transfer(1))
    for k, x in enumerate(lefts(real, imag)):
        tail[k] = x
    each(1, count, lambda k: send(k).wait())
    index_ref[...] = out_ref[...].astype(jnp.int32)


def main_kernel(
    own_layers, index_ref, gathered, theta_ref, picked, scale, head, tail, weights, start,
    fields, gradient, index, cosines, sines, kept, slopes, index_sem, slope_sem, out_sem,
):
    index_copy = pltpu.make_async_copy(index_ref, index, index_sem)
    index_copy.start()
    here = lax.axis_index("sect")
    sections = gathered.shape[0]
    layers = sections * own_layers
    mon, harm = picked.shape
    first = here * own_layers
    last = first + 1
    theta = theta_ref[...]

    depths = gathered[:, 0, :]
    for t in range(own_layers):
        turn = depths[:, own_layers + t : own_layers + t + 1] * theta
        cosines[t], sines[t] = turns_of(turn)

    index_copy.wait()

    def step(layer, real, imag, form=product):
        section, t = layer // own_layers, lax.rem(layer, own_layers)
        cos, sin = cosines[t, pl.ds(section, 1), :], sines[t, pl.ds(section, 1), :]
        n = index[section, 0, t]
        return form(
            cos * real - sin * imag, cos * imag + sin * real,
            (weights[n, 0], weights[n, 1], weights[n, 2]),
        )

    def pairs(count, one, two, state, form):
        done = 0
        for size in UNROLL:
            def several(i, c, size=size, done=done):
                for j in range(size):
                    k = done + size * i + j
                    c = step(one - k, c[0], c[1], form) + step(two - k, c[2], c[3])
                return c

            times = (count - done) // size
            state = lax.fori_loop(0, times, several, state)
            done = done + times * size
        return state

    rows = lax.broadcasted_iota(jnp.int32, (harm, harm), 0)
    columns = lax.broadcasted_iota(jnp.int32, (harm, harm), 1)
    unit = jnp.where(rows == columns, 1.0, 0.0).astype(f32)
    none = jnp.zeros((harm, harm), f32)

    half = (layers - first - own_layers) // 2
    row_real, row_imag, sub_real, sub_imag = pairs(
        half, layers - 1, layers - 1 - half, (picked[...], jnp.zeros((mon, harm), f32), unit, none),
        product_rows,
    )
    half = first // 2
    top_real, top_imag, real, imag = pairs(
        half, first - 1, half - 1, (head[0], head[1], unit, none), product
    )

    real, imag = product(real, imag, (start[0], start[1], start[2]))
    row_real, row_imag = product(row_real, row_imag, rights(sub_real, sub_imag))
    real, imag = product(top_real, top_imag, rights(real, imag))
    kept[0, 0], kept[0, 1] = real, imag

    def out(j, r):
        return pltpu.make_async_copy(kept.at[j, r], fields.at[j, 0, :, r, :], out_sem.at[j, r])

    out(0, 0).start()
    out(0, 1).start()
    two_real = jnp.concatenate([row_real, row_real * theta], axis=0)
    two_imag = jnp.concatenate([row_imag, row_imag * theta], axis=0)
    two_real, two_imag = step(last, two_real, two_imag, product_rows)
    two_real = jnp.concatenate([two_real[:mon] * theta, two_real], axis=0)
    two_imag = jnp.concatenate([two_imag[:mon] * theta, two_imag], axis=0)
    operands = [
        jnp.concatenate([tail[k], x], axis=0) for k, x in enumerate(lefts(two_real, two_imag))
    ]
    real, imag = multiply(operands, rights(real, imag))
    kept[1, 0], kept[1, 1] = real[:harm], imag[:harm]
    out(1, 0).start()
    out(1, 1).start()
    at = tail.shape[1]
    strength = scale[...]
    seen_real, seen_imag = real[at + mon : at + 2 * mon] * strength, imag[at + mon : at + 2 * mon] * strength
    totals = [
        jnp.sum(
            seen_real * imag[top : top + mon] - seen_imag * real[top : top + mon],
            axis=(0, 1), keepdims=True,
        )
        for top in (at, at + 2 * mon)
    ]
    slopes[...] = -2.0 * jnp.concatenate(totals, axis=1)
    slope_copy = pltpu.make_async_copy(slopes, gradient, slope_sem)
    slope_copy.start()
    for j in range(2):
        out(j, 0).wait()
        out(j, 1).wait()
    slope_copy.wait()


def local(pattern, thickness, coupling, angles, points, incident, monitors, weights):
    sections = lax.axis_size("sect")
    own_layers = pattern.shape[0]
    assert own_layers == 2
    patterns, harm = coupling.shape[0], incident.shape[-1]
    layers = sections * own_layers
    depth = depth_of(harm)
    vmem = pl.BlockSpec(memory_space=pltpu.VMEM)
    hbm = pl.BlockSpec(memory_space=pltpu.HBM)
    mon = monitors.shape[0]
    *tables, prepared, start = pl.pallas_call(
        functools.partial(gather_kernel, sections),
        out_shape=(
            jax.ShapeDtypeStruct((sections, 1, LANES), f32),
            jax.ShapeDtypeStruct((sections, 1, LANES), jnp.int32),
            jax.ShapeDtypeStruct((1, harm), f32),
            jax.ShapeDtypeStruct((mon, harm), f32),
            jax.ShapeDtypeStruct((mon, harm), f32),
            jax.ShapeDtypeStruct((2, harm, harm), f32),
            jax.ShapeDtypeStruct((3, harm + -harm % 16, depth), bf16),
            jax.ShapeDtypeStruct((patterns, 3, depth, harm), bf16),
            jax.ShapeDtypeStruct((3, depth, harm), bf16),
        ),
        in_specs=[hbm] * 7 + [vmem],
        out_specs=(vmem,) * 9,
        scratch_shapes=[
            pltpu.SMEM((own_layers,), jnp.int32),
            pltpu.SMEM((own_layers,), f32),
            pltpu.VMEM(angles.shape, f32),
            pltpu.SMEM((mon,), jnp.int32),
            pltpu.SMEM((mon,), f32),
            pltpu.VMEM((1, LANES), f32),
            pltpu.VMEM((2, harm, harm), f32),
            pltpu.VMEM((patterns, 2, harm, harm), f32),
            pltpu.SemaphoreType.DMA((5,)),
            pltpu.SemaphoreType.DMA((sections,)),
            pltpu.SemaphoreType.DMA((sections,)),
            pltpu.SemaphoreType.DMA((patterns, 2)),
            pltpu.SemaphoreType.DMA((2,)),
        ],
        compiler_params=pltpu.CompilerParams(
            collective_id=0, has_side_effects=True, vmem_limit_bytes=14 * 2**20
        ),
    )(
        *(
            pltpu.with_memory_space_constraint(x, pltpu.HBM)
            for x in (
                pattern, thickness, angles, monitors, weights,
                coupling.transpose(0, 2, 1, 3), incident.transpose(0, 2, 1, 3),
            )
        ),
        points[None],
    )
    gathered, index, theta, picked, scale, head, tail = tables
    fields, gradient = pl.pallas_call(
        functools.partial(main_kernel, own_layers),
        out_shape=(
            jax.ShapeDtypeStruct((own_layers, 1, harm, 2, harm), f32),
            jax.ShapeDtypeStruct((1, own_layers), f32),
        ),
        in_specs=[vmem] * 9,
        out_specs=(hbm, hbm),
        scratch_shapes=[
            pltpu.SMEM((sections, 1, LANES), jnp.int32),
            pltpu.VMEM((own_layers, sections, harm), f32),
            pltpu.VMEM((own_layers, sections, harm), f32),
            pltpu.VMEM((2, 2, harm, harm), f32),
            pltpu.VMEM((1, own_layers), f32),
            pltpu.SemaphoreType.DMA,
            pltpu.SemaphoreType.DMA,
            pltpu.SemaphoreType.DMA((2, 2)),
        ],
        compiler_params=pltpu.CompilerParams(vmem_limit_bytes=16 * 2**20),
    )(index, gathered, theta, picked, scale, head, tail, prepared, start)
    return fields.transpose(0, 1, 3, 2, 4), gradient


def solution(mesh):
    in_specs = (
        P("sect"), P("sect"), P(), P(), P("groups"),
        P("groups", None, None, None), P(), P(),
    )
    out_specs = (P("sect", "groups", None, None, None), P("groups", "sect"))
    return jax.shard_map(local, mesh=mesh, in_specs=in_specs, out_specs=out_specs, check_vma=False)
```

```python
import functools
import math
import jax
import jax.numpy as jnp
from jax import lax
from jax.experimental import pallas as pl
from jax.experimental.pallas import tpu as pltpu
from jax.sharding import PartitionSpec as P

norm_scale = (1.0 + 1.0 / 22.0) ** (-0.5)
f32 = jnp.float32
bf16 = jnp.bfloat16
LANES = 128
UNROLL = (5, 2, 1)


def cut_of(harm):
    cut = harm // LANES * LANES
    rest = harm - cut
    assert 3 * rest <= LANES
    return cut, rest


def split(x):
    hi = x.astype(bf16)
    return hi, (x - hi.astype(f32)).astype(bf16)


def depth_of(harm):
    return 3 * cut_of(harm)[0] + LANES


def left(x):
    cut, rest = cut_of(x.shape[1])
    hi, lo = split(x)
    a, b = hi[:, cut:], lo[:, cut:]
    zero = jnp.zeros((x.shape[0], LANES - 3 * rest), bf16)
    return jnp.concatenate([hi[:, :cut], lo[:, :cut], hi[:, :cut], a, b, a, zero], axis=1)


def right_parts(x):
    cut, rest = cut_of(x.shape[0])
    hi = x.astype(bf16)
    wide = hi.astype(f32)
    lo = x - wide
    zero = jnp.zeros((LANES - 3 * rest, x.shape[1]), f32)
    tail = jnp.concatenate([wide[cut:], wide[cut:], lo[cut:], zero], axis=0)
    return hi[:cut], lo[:cut].astype(bf16), tail.astype(bf16)


def right(x):
    hi, lo, tail = right_parts(x)
    return jnp.concatenate([hi, hi, lo, tail], axis=0)


def rights(real, imag):
    return [right(real), right(imag - real), right(real + imag)]


def dot(a, b):
    return lax.dot_general(a, b, (((1,), (0,)), ((), ())), preferred_element_type=f32)


def lefts(real, imag):
    return left(real + imag), left(real), left(imag)


def multiply(operands, weights):
    both, first, second = (dot(x, y) for x, y in zip(operands, weights))
    return both - second, both + first


def product(real, imag, weights):
    return multiply(lefts(real, imag), weights)


def product_rows(real, imag, weights):
    m = real.shape[0]
    both = left(jnp.concatenate([real + imag, real - imag], axis=0))
    low, high = dot(both, weights[1]), dot(both, weights[2])
    return 0.5 * (high[m:] - low[:m]), 0.5 * (high[:m] + low[m:])


def turns_of(x):
    k = jnp.floor(x * (2.0 / math.pi) + 0.5)
    r = ((x - k * 1.5703125) - k * 4.837512969970703e-4) - k * 7.549789948768648e-8
    z = r * r
    sin = r + r * z * (-1.6666654611e-1 + z * (8.3321608736e-3 + z * -1.9515295891e-4))
    cos = 1.0 - 0.5 * z + z * z * (
        4.166664568298827e-2 + z * (-1.388731625493765e-3 + z * 2.443315711809948e-5)
    )
    q = k.astype(jnp.int32) & 3
    odd = (q & 1) == 1
    cos, sin = jnp.where(odd, sin, cos), jnp.where(odd, cos, sin)
    cos = jnp.where((q == 1) | (q == 2), -cos, cos)
    sin = jnp.where(q >= 2, -sin, sin)
    return norm_scale * cos, norm_scale * sin


def store_right(ref, at, x):
    hi, lo, tail = right_parts(x)
    cut = hi.shape[0]
    ref[at + (pl.ds(0, cut),)] = hi
    ref[at + (pl.ds(cut, cut),)] = hi
    ref[at + (pl.ds(2 * cut, cut),)] = lo
    ref[at + (pl.ds(3 * cut, LANES),)] = tail


def each(low, high, act):
    if high - low <= 16:
        for k in range(low, high):
            act(k)
    else:
        lax.fori_loop(low, high, lambda k, c: (act(k), c)[1], 0)


def gather_kernel(
    count, pattern, thickness, angles, monitors, strengths, coupling, incident, points,
    out_ref, index_ref, theta_ref, picked_ref, scale_ref, head, tail, weights, start,
    own_pattern, own_thickness, own_angles, own_monitors, own_strengths, own_ref, waves, mixing,
    own_sem, send_sem, recv_sem, load_sem, wave_sem,
):
    here = lax.axis_index("sect")
    barrier = pltpu.get_barrier_semaphore()
    patterns = coupling.shape[0]
    harm = coupling.shape[-1]
    own_layers = pattern.shape[0]
    mesh_id = pl.DeviceIdType.MESH

    def peer(k):
        return lax.rem(here + k, count)

    def greet(k):
        pl.semaphore_signal(barrier, inc=1, device_id={"sect": peer(k)}, device_id_type=mesh_id)

    own_copies = [
        pltpu.make_async_copy(source, target, own_sem.at[k])
        for k, (source, target) in enumerate((
            (pattern, own_pattern), (thickness, own_thickness), (angles, own_angles),
            (monitors, own_monitors), (strengths, own_strengths),
        ))
    ]
    for copy in own_copies:
        copy.start()
    each(1, count, greet)

    bunch = 4 if patterns % 4 == 0 else 1
    bunches = patterns // bunch

    def load(b, r):
        some = pl.ds(b * bunch, bunch)
        return pltpu.make_async_copy(coupling.at[some, :, r, :], mixing.at[some, r], load_sem.at[b, r])

    def load_start(b, c):
        load(b, 0).start()
        load(b, 1).start()
        return c

    lax.fori_loop(0, bunches, load_start, 0)
    wave = [
        pltpu.make_async_copy(incident.at[0, :, r, :], waves.at[r], wave_sem.at[r]) for r in range(2)
    ]
    for copy in wave:
        copy.start()

    for copy in own_copies[:2]:
        copy.wait()
    lanes = lax.broadcasted_iota(jnp.int32, (1, LANES), 1)
    own = jnp.zeros((1, LANES), f32)
    for j in range(own_layers):
        own = jnp.where(lanes == j, own_pattern[j].astype(f32), own)
        own = jnp.where(lanes == own_layers + j, own_thickness[j], own)
    own_ref[...] = own
    out_ref[here] = own
    rows = lax.broadcasted_iota(jnp.int32, (harm, harm), 0)
    columns = lax.broadcasted_iota(jnp.int32, (harm, harm), 1)
    unit = jnp.where(rows == columns, 1.0, 0.0).astype(f32)

    def prepare_one(n, c):
        real, imag = unit + mixing[n, 0], mixing[n, 1]
        store_right(weights, (n, 0), real)
        store_right(weights, (n, 1), imag - real)
        store_right(weights, (n, 2), real + imag)
        return c

    def prepare(b, c):
        load(b, 0).wait()
        load(b, 1).wait()
        return lax.fori_loop(b * bunch, (b + 1) * bunch, prepare_one, c)

    early = jnp.where(here < 2, bunches // 2, jnp.where(here < count // 2, bunches // 4, 0))
    lax.fori_loop(0, early, prepare, 0)
    pl.semaphore_wait(barrier, count - 1)

    def send(k):
        return pltpu.make_async_remote_copy(
            src_ref=own_ref,
            dst_ref=out_ref.at[here],
            send_sem=send_sem.at[k],
            recv_sem=recv_sem.at[k],
            device_id={"sect": peer(k)},
            device_id_type=mesh_id,
        )

    each(1, count, lambda k: send(k).start())

    for copy in own_copies[2:]:
        copy.wait()
    entries = lax.broadcasted_iota(jnp.int32, own_angles.shape, 0)
    theta = jnp.sum(jnp.where(entries == points[...], own_angles[...], 0.0), axis=0, keepdims=True)
    theta_ref[...] = theta
    mon = monitors.shape[0]
    pick_rows = lax.broadcasted_iota(jnp.int32, (mon, harm), 0)
    pick_lanes = lax.broadcasted_iota(jnp.int32, (mon, harm), 1)
    picked = jnp.zeros((mon, harm), f32)
    scale = jnp.zeros((mon, harm), f32)
    for m in range(mon):
        picked = jnp.where((pick_rows == m) & (pick_lanes == own_monitors[m]), 1.0, picked)
        scale = jnp.where(pick_rows == m, own_strengths[m], scale)
    picked_ref[...] = picked
    scale_ref[...] = scale * (1.0 / harm)
    turns = jnp.concatenate([theta * own_thickness[j] for j in range(own_layers)], axis=0)
    turns = jnp.concatenate([*turns_of(turns), jnp.zeros((8 - 2 * own_layers, harm), f32)], axis=0).T

    lax.fori_loop(early, bunches, prepare, 0)
    for copy in wave:
        copy.wait()
    real, imag = waves[0], waves[1]
    store_right(start, (0,), real)
    store_right(start, (1,), imag - real)
    store_right(start, (2,), real + imag)

    def transfer(j):
        cos, sin = turns[:, j : j + 1], turns[:, own_layers + j : own_layers + j + 1]
        n = own_pattern[j]
        real, imag = unit + mixing[n, 0], mixing[n, 1]
        return cos * real - sin * imag, cos * imag + sin * real

    head[0], head[1] = transfer(0)
    gap = jnp.zeros((-harm % 16, harm), f32)
    real, imag = (jnp.concatenate([x, gap], axis=0) for x in transfer(1))
    for k, x in enumerate(lefts(real, imag)):
        tail[k] = x
    each(1, count, lambda k: send(k).wait())
    index_ref[...] = out_ref[...].astype(jnp.int32)


def main_kernel(
    own_layers, index_ref, gathered, theta_ref, picked, scale, head, tail, weights, start,
    fields, gradient, index, cosines, sines, kept, slopes, row_state, sub_state, pair_state, slope_sem, out_sem,
):
    here = lax.axis_index("sect")
    sections = gathered.shape[0]
    layers = sections * own_layers
    mon, harm = picked.shape
    first = here * own_layers
    last = first + 1
    theta = theta_ref[...]

    depths = gathered[:, 0, :]
    for t in range(own_layers):
        turn = depths[:, own_layers + t : own_layers + t + 1] * theta
        cosines[t], sines[t] = turns_of(turn)

    def note(j, c):
        row = index_ref[j]
        for t in range(own_layers):
            index[j * own_layers + t] = row[0, t]
        return c

    lax.fori_loop(0, sections, note, 0, unroll=8)

    def step(layer, real, imag, form=product):
        section, t = layer // own_layers, lax.rem(layer, own_layers)
        cos, sin = cosines[t, pl.ds(section, 1), :], sines[t, pl.ds(section, 1), :]
        n = index[layer]
        return form(
            cos * real - sin * imag, cos * imag + sin * real,
            (weights[n, 0], weights[n, 1], weights[n, 2]),
        )

    def move(state, layer, form):
        state[0], state[1] = step(layer, state[0], state[1], form)

    def loop(count, body):
        done = 0
        for size in UNROLL:
            def several(i, c, size=size, done=done):
                for j in range(size):
                    body(done + size * i + j)
                return c

            times = (count - done) // size
            lax.fori_loop(0, times, several, 0)
            done = done + times * size

    rows = lax.broadcasted_iota(jnp.int32, (harm, harm), 0)
    columns = lax.broadcasted_iota(jnp.int32, (harm, harm), 1)
    unit = jnp.where(rows == columns, 1.0, 0.0).astype(f32)
    none = jnp.zeros((harm, harm), f32)
    top, low = pair_state.at[pl.ds(0, 2)], pair_state.at[pl.ds(2, 2)]

    row_state[0], row_state[1] = picked[...], jnp.zeros((mon, harm), f32)
    upper, under = sub_state.at[pl.ds(0, 2)], sub_state.at[pl.ds(2, 2)]
    upper[0], upper[1] = unit, none
    under[0], under[1] = unit, none
    top[0], top[1] = head[0], head[1]
    low[0], low[1] = unit, none
    behind = layers - first - own_layers
    third = behind // 3
    high = layers - 1 - (behind - 2 * third)

    def suffix(k):
        move(upper, high - k, product)
        move(under, high - third - k, product)
        move(row_state, layers - 1 - k, product_rows)

    def suffix_rest(k, c):
        move(row_state, layers - 1 - third - k, product_rows)
        return c

    loop(third, suffix)
    lax.fori_loop(0, behind - 3 * third, suffix_rest, 0)

    def prefix(k):
        move(top, first - 1 - k, product)
        move(low, first // 2 - 1 - k, product)

    loop(first // 2, prefix)

    real, imag = product(low[0], low[1], (start[0], start[1], start[2]))
    row_real, row_imag = product_rows(row_state[0], row_state[1], rights(upper[0], upper[1]))
    real, imag = product(top[0], top[1], rights(real, imag))
    row_real, row_imag = product_rows(row_real, row_imag, rights(under[0], under[1]))
    kept[0, 0], kept[0, 1] = real, imag

    def out(j, r):
        return pltpu.make_async_copy(kept.at[j, r], fields.at[j, 0, :, r, :], out_sem.at[j, r])

    out(0, 0).start()
    out(0, 1).start()
    two_real = jnp.concatenate([row_real, row_real * theta], axis=0)
    two_imag = jnp.concatenate([row_imag, row_imag * theta], axis=0)
    two_real, two_imag = step(last, two_real, two_imag, product_rows)
    two_real = jnp.concatenate([two_real[:mon] * theta, two_real], axis=0)
    two_imag = jnp.concatenate([two_imag[:mon] * theta, two_imag], axis=0)
    operands = [
        jnp.concatenate([tail[k], x], axis=0) for k, x in enumerate(lefts(two_real, two_imag))
    ]
    real, imag = multiply(operands, rights(real, imag))
    kept[1, 0], kept[1, 1] = real[:harm], imag[:harm]
    out(1, 0).start()
    out(1, 1).start()
    at = tail.shape[1]
    strength = scale[...]
    seen_real, seen_imag = real[at + mon : at + 2 * mon] * strength, imag[at + mon : at + 2 * mon] * strength
    totals = [
        jnp.sum(
            seen_real * imag[top : top + mon] - seen_imag * real[top : top + mon],
            axis=(0, 1), keepdims=True,
        )
        for top in (at, at + 2 * mon)
    ]
    slopes[...] = -2.0 * jnp.concatenate(totals, axis=1)
    slope_copy = pltpu.make_async_copy(slopes, gradient, slope_sem)
    slope_copy.start()
    for j in range(2):
        out(j, 0).wait()
        out(j, 1).wait()
    slope_copy.wait()


def local(pattern, thickness, coupling, angles, points, incident, monitors, weights):
    sections = lax.axis_size("sect")
    own_layers = pattern.shape[0]
    assert own_layers == 2
    patterns, harm = coupling.shape[0], incident.shape[-1]
    layers = sections * own_layers
    depth = depth_of(harm)
    vmem = pl.BlockSpec(memory_space=pltpu.VMEM)
    hbm = pl.BlockSpec(memory_space=pltpu.HBM)
    mon = monitors.shape[0]
    *tables, prepared, start = pl.pallas_call(
        functools.partial(gather_kernel, sections),
        out_shape=(
            jax.ShapeDtypeStruct((sections, 1, LANES), f32),
            jax.ShapeDtypeStruct((sections, 1, LANES), jnp.int32),
            jax.ShapeDtypeStruct((1, harm), f32),
            jax.ShapeDtypeStruct((mon, harm), f32),
            jax.ShapeDtypeStruct((mon, harm), f32),
            jax.ShapeDtypeStruct((2, harm, harm), f32),
            jax.ShapeDtypeStruct((3, harm + -harm % 16, depth), bf16),
            jax.ShapeDtypeStruct((patterns, 3, depth, harm), bf16),
            jax.ShapeDtypeStruct((3, depth, harm), bf16),
        ),
        in_specs=[hbm] * 7 + [vmem],
        out_specs=(vmem,) * 9,
        scratch_shapes=[
            pltpu.SMEM((own_layers,), jnp.int32),
            pltpu.SMEM((own_layers,), f32),
            pltpu.VMEM(angles.shape, f32),
            pltpu.SMEM((mon,), jnp.int32),
            pltpu.SMEM((mon,), f32),
            pltpu.VMEM((1, LANES), f32),
            pltpu.VMEM((2, harm, harm), f32),
            pltpu.VMEM((patterns, 2, harm, harm), f32),
            pltpu.SemaphoreType.DMA((5,)),
            pltpu.SemaphoreType.DMA((sections,)),
            pltpu.SemaphoreType.DMA((sections,)),
            pltpu.SemaphoreType.DMA((patterns, 2)),
            pltpu.SemaphoreType.DMA((2,)),
        ],
        compiler_params=pltpu.CompilerParams(
            collective_id=0, has_side_effects=True, vmem_limit_bytes=14 * 2**20
        ),
    )(
        *(
            pltpu.with_memory_space_constraint(x, pltpu.HBM)
            for x in (
                pattern, thickness, angles, monitors, weights,
                coupling.transpose(0, 2, 1, 3), incident.transpose(0, 2, 1, 3),
            )
        ),
        points[None],
    )
    gathered, index, theta, picked, scale, head, tail = tables
    fields, gradient = pl.pallas_call(
        functools.partial(main_kernel, own_layers),
        out_shape=(
            jax.ShapeDtypeStruct((own_layers, 1, harm, 2, harm), f32),
            jax.ShapeDtypeStruct((1, own_layers), f32),
        ),
        in_specs=[vmem] * 9,
        out_specs=(hbm, hbm),
        scratch_shapes=[
            pltpu.SMEM((layers,), jnp.int32),
            pltpu.VMEM((own_layers, sections, harm), f32),
            pltpu.VMEM((own_layers, sections, harm), f32),
            pltpu.VMEM((2, 2, harm, harm), f32),
            pltpu.VMEM((1, own_layers), f32),
            pltpu.VMEM((2, mon, harm), f32),
            pltpu.VMEM((4, harm, harm), f32),
            pltpu.VMEM((4, harm, harm), f32),
            pltpu.SemaphoreType.DMA,
            pltpu.SemaphoreType.DMA((2, 2)),
        ],
        compiler_params=pltpu.CompilerParams(vmem_limit_bytes=16 * 2**20),
    )(index, gathered, theta, picked, scale, head, tail, prepared, start)
    return fields.transpose(0, 1, 3, 2, 4), gradient


def solution(mesh):
    in_specs = (
        P("sect"), P("sect"), P(), P(), P("groups"),
        P("groups", None, None, None), P(), P(),
    )
    out_specs = (P("sect", "groups", None, None, None), P("groups", "sect"))
    return jax.shard_map(local, mesh=mesh, in_specs=in_specs, out_specs=out_specs, check_vma=False)
```

```python
import functools
import math
import jax
import jax.numpy as jnp
from jax import lax
from jax.experimental import pallas as pl
from jax.experimental.pallas import tpu as pltpu
from jax.sharding import PartitionSpec as P

norm_scale = (1.0 + 1.0 / 22.0) ** (-0.5)
f32 = jnp.float32
bf16 = jnp.bfloat16
LANES = 128
UNROLL = (5, 2, 1)


def cut_of(harm):
    cut = harm // LANES * LANES
    rest = harm - cut
    assert 3 * rest <= LANES
    return cut, rest


def split(x):
    hi = x.astype(bf16)
    return hi, (x - hi.astype(f32)).astype(bf16)


def depth_of(harm):
    return 3 * cut_of(harm)[0] + LANES


def left(x):
    cut, rest = cut_of(x.shape[1])
    hi, lo = split(x)
    a, b = hi[:, cut:], lo[:, cut:]
    zero = jnp.zeros((x.shape[0], LANES - 3 * rest), bf16)
    return jnp.concatenate([hi[:, :cut], lo[:, :cut], hi[:, :cut], a, b, a, zero], axis=1)


def right_parts(x):
    cut, rest = cut_of(x.shape[0])
    hi = x.astype(bf16)
    wide = hi.astype(f32)
    lo = x - wide
    zero = jnp.zeros((LANES - 3 * rest, x.shape[1]), f32)
    tail = jnp.concatenate([wide[cut:], wide[cut:], lo[cut:], zero], axis=0)
    return hi[:cut], lo[:cut].astype(bf16), tail.astype(bf16)


def right(x):
    hi, lo, tail = right_parts(x)
    return jnp.concatenate([hi, hi, lo, tail], axis=0)


def rights(real, imag):
    return [right(real), right(imag - real), right(real + imag)]


def dot(a, b):
    return lax.dot_general(a, b, (((1,), (0,)), ((), ())), preferred_element_type=f32)


def lefts(real, imag):
    return left(real + imag), left(real), left(imag)


def multiply(operands, weights):
    both, first, second = (dot(x, y) for x, y in zip(operands, weights))
    return both - second, both + first


def product(real, imag, weights):
    return multiply(lefts(real, imag), weights)


def product_rows(real, imag, weights):
    m = real.shape[0]
    both = left(jnp.concatenate([real + imag, real - imag], axis=0))
    low, high = dot(both, weights[1]), dot(both, weights[2])
    return 0.5 * (high[m:] - low[:m]), 0.5 * (high[:m] + low[m:])


def turns_of(x):
    k = jnp.floor(x * (2.0 / math.pi) + 0.5)
    r = ((x - k * 1.5703125) - k * 4.837512969970703e-4) - k * 7.549789948768648e-8
    z = r * r
    sin = r + r * z * (-1.6666654611e-1 + z * (8.3321608736e-3 + z * -1.9515295891e-4))
    cos = 1.0 - 0.5 * z + z * z * (
        4.166664568298827e-2 + z * (-1.388731625493765e-3 + z * 2.443315711809948e-5)
    )
    q = k.astype(jnp.int32) & 3
    odd = (q & 1) == 1
    cos, sin = jnp.where(odd, sin, cos), jnp.where(odd, cos, sin)
    cos = jnp.where((q == 1) | (q == 2), -cos, cos)
    sin = jnp.where(q >= 2, -sin, sin)
    return norm_scale * cos, norm_scale * sin


def store_right(ref, at, x):
    hi, lo, tail = right_parts(x)
    cut = hi.shape[0]
    ref[at + (pl.ds(0, cut),)] = hi
    ref[at + (pl.ds(cut, cut),)] = hi
    ref[at + (pl.ds(2 * cut, cut),)] = lo
    ref[at + (pl.ds(3 * cut, LANES),)] = tail


def each(low, high, act):
    if high - low <= 16:
        for k in range(low, high):
            act(k)
    else:
        lax.fori_loop(low, high, lambda k, c: (act(k), c)[1], 0)


def gather_kernel(
    count, pattern, thickness, angles, monitors, strengths, coupling, incident, points,
    out_ref, index_ref, theta_ref, picked_ref, scale_ref, head, tail, weights, start,
    own_pattern, own_thickness, own_angles, own_monitors, own_strengths, own_point, own_ref, waves, mixing,
    own_sem, send_sem, recv_sem, load_sem, wave_sem,
):
    here = lax.axis_index("sect")
    barrier = pltpu.get_barrier_semaphore()
    patterns = coupling.shape[0]
    harm = coupling.shape[-1]
    own_layers = pattern.shape[0]
    mesh_id = pl.DeviceIdType.MESH

    def peer(k):
        return lax.rem(here + k, count)

    def greet(k):
        pl.semaphore_signal(barrier, inc=1, device_id={"sect": peer(k)}, device_id_type=mesh_id)

    own_copies = [
        pltpu.make_async_copy(source, target, own_sem.at[k])
        for k, (source, target) in enumerate((
            (pattern, own_pattern), (thickness, own_thickness), (angles, own_angles),
            (monitors, own_monitors), (strengths, own_strengths), (points, own_point),
        ))
    ]
    for copy in own_copies:
        copy.start()
    each(1, count, greet)

    bunch = 4 if patterns % 4 == 0 else 1
    bunches = patterns // bunch

    def load(b, r):
        some = pl.ds(b * bunch, bunch)
        return pltpu.make_async_copy(coupling.at[some, :, r, :], mixing.at[some, r], load_sem.at[b, r])

    def load_start(b, c):
        load(b, 0).start()
        load(b, 1).start()
        return c

    lax.fori_loop(0, bunches, load_start, 0)
    wave = [
        pltpu.make_async_copy(incident.at[0, :, r, :], waves.at[r], wave_sem.at[r]) for r in range(2)
    ]
    for copy in wave:
        copy.start()

    for copy in own_copies[:2]:
        copy.wait()
    lanes = lax.broadcasted_iota(jnp.int32, (1, LANES), 1)
    own = jnp.zeros((1, LANES), f32)
    for j in range(own_layers):
        own = jnp.where(lanes == j, own_pattern[j].astype(f32), own)
        own = jnp.where(lanes == own_layers + j, own_thickness[j], own)
    own_ref[...] = own
    out_ref[here] = own
    rows = lax.broadcasted_iota(jnp.int32, (harm, harm), 0)
    columns = lax.broadcasted_iota(jnp.int32, (harm, harm), 1)
    unit = jnp.where(rows == columns, 1.0, 0.0).astype(f32)

    def prepare_one(n, c):
        real, imag = unit + mixing[n, 0], mixing[n, 1]
        store_right(weights, (n, 0), real)
        store_right(weights, (n, 1), imag - real)
        store_right(weights, (n, 2), real + imag)
        return c

    def prepare(b, c):
        load(b, 0).wait()
        load(b, 1).wait()
        return lax.fori_loop(b * bunch, (b + 1) * bunch, prepare_one, c)

    early = jnp.where(here < 2, bunches // 2, jnp.where(here < count // 2, bunches // 4, 0))
    lax.fori_loop(0, early, prepare, 0)
    pl.semaphore_wait(barrier, count - 1)

    def send(k):
        return pltpu.make_async_remote_copy(
            src_ref=own_ref,
            dst_ref=out_ref.at[here],
            send_sem=send_sem.at[k],
            recv_sem=recv_sem.at[k],
            device_id={"sect": peer(k)},
            device_id_type=mesh_id,
        )

    each(1, count, lambda k: send(k).start())

    for copy in own_copies[2:]:
        copy.wait()
    entries = lax.broadcasted_iota(jnp.int32, own_angles.shape, 0)
    theta = jnp.sum(jnp.where(entries == own_point[...], own_angles[...], 0.0), axis=0, keepdims=True)
    theta_ref[...] = theta
    mon = monitors.shape[0]
    pick_rows = lax.broadcasted_iota(jnp.int32, (mon, harm), 0)
    pick_lanes = lax.broadcasted_iota(jnp.int32, (mon, harm), 1)
    picked = jnp.zeros((mon, harm), f32)
    scale = jnp.zeros((mon, harm), f32)
    for m in range(mon):
        picked = jnp.where((pick_rows == m) & (pick_lanes == own_monitors[m]), 1.0, picked)
        scale = jnp.where(pick_rows == m, own_strengths[m], scale)
    picked_ref[...] = picked
    scale_ref[...] = scale * (1.0 / harm)
    turns = jnp.concatenate([theta * own_thickness[j] for j in range(own_layers)], axis=0)
    turns = jnp.concatenate([*turns_of(turns), jnp.zeros((8 - 2 * own_layers, harm), f32)], axis=0).T

    lax.fori_loop(early, bunches, prepare, 0)
    for copy in wave:
        copy.wait()
    real, imag = waves[0], waves[1]
    store_right(start, (0,), real)
    store_right(start, (1,), imag - real)
    store_right(start, (2,), real + imag)

    def transfer(j):
        cos, sin = turns[:, j : j + 1], turns[:, own_layers + j : own_layers + j + 1]
        n = own_pattern[j]
        real, imag = unit + mixing[n, 0], mixing[n, 1]
        return cos * real - sin * imag, cos * imag + sin * real

    head[0], head[1] = transfer(0)
    gap = jnp.zeros((-harm % 16, harm), f32)
    real, imag = (jnp.concatenate([x, gap], axis=0) for x in transfer(1))
    for k, x in enumerate(lefts(real, imag)):
        tail[k] = x
    each(1, count, lambda k: send(k).wait())
    index_ref[...] = out_ref[...].astype(jnp.int32)


def main_kernel(
    own_layers, index_ref, gathered, theta_ref, picked, scale, head, tail, weights, start,
    fields, gradient, index, cosines, sines, kept, slopes, row_state, sub_state, pair_state, slope_sem, out_sem,
):
    here = lax.axis_index("sect")
    sections = gathered.shape[0]
    layers = sections * own_layers
    mon, harm = picked.shape
    first = here * own_layers
    last = first + 1
    theta = theta_ref[...]

    depths = gathered[:, 0, :]
    for t in range(own_layers):
        turn = depths[:, own_layers + t : own_layers + t + 1] * theta
        cosines[t], sines[t] = turns_of(turn)

    def note(j, c):
        row = index_ref[j]
        for t in range(own_layers):
            index[j * own_layers + t] = row[0, t]
        return c

    lax.fori_loop(0, sections, note, 0, unroll=16)

    def step(layer, real, imag, form=product):
        section, t = layer // own_layers, lax.rem(layer, own_layers)
        cos, sin = cosines[t, pl.ds(section, 1), :], sines[t, pl.ds(section, 1), :]
        n = index[layer]
        return form(
            cos * real - sin * imag, cos * imag + sin * real,
            (weights[n, 0], weights[n, 1], weights[n, 2]),
        )

    def move(state, layer, form):
        state[0], state[1] = step(layer, state[0], state[1], form)

    def loop(count, body):
        done = 0
        for size in UNROLL:
            def several(i, c, size=size, done=done):
                for j in range(size):
                    body(done + size * i + j)
                return c

            times = (count - done) // size
            lax.fori_loop(0, times, several, 0)
            done = done + times * size

    rows = lax.broadcasted_iota(jnp.int32, (harm, harm), 0)
    columns = lax.broadcasted_iota(jnp.int32, (harm, harm), 1)
    unit = jnp.where(rows == columns, 1.0, 0.0).astype(f32)
    none = jnp.zeros((harm, harm), f32)
    top, low = pair_state.at[pl.ds(0, 2)], pair_state.at[pl.ds(2, 2)]

    row_state[0], row_state[1] = picked[...], jnp.zeros((mon, harm), f32)
    upper, under = sub_state.at[pl.ds(0, 2)], sub_state.at[pl.ds(2, 2)]
    upper[0], upper[1] = unit, none
    under[0], under[1] = unit, none
    top[0], top[1] = head[0], head[1]
    low[0], low[1] = unit, none
    behind = layers - first - own_layers
    third = behind // 3
    high = layers - 1 - (behind - 2 * third)

    def suffix(k):
        move(upper, high - k, product)
        move(under, high - third - k, product)
        move(row_state, layers - 1 - k, product_rows)

    def suffix_rest(k, c):
        move(row_state, layers - 1 - third - k, product_rows)
        return c

    loop(third, suffix)
    lax.fori_loop(0, behind - 3 * third, suffix_rest, 0)

    def prefix(k):
        move(top, first - 1 - k, product)
        move(low, first // 2 - 1 - k, product)

    loop(first // 2, prefix)

    real, imag = product(low[0], low[1], (start[0], start[1], start[2]))
    row_real, row_imag = product_rows(row_state[0], row_state[1], rights(upper[0], upper[1]))
    real, imag = product(top[0], top[1], rights(real, imag))
    row_real, row_imag = product_rows(row_real, row_imag, rights(under[0], under[1]))
    kept[0, 0], kept[0, 1] = real, imag

    def out(j, r):
        return pltpu.make_async_copy(kept.at[j, r], fields.at[j, 0, :, r, :], out_sem.at[j, r])

    out(0, 0).start()
    out(0, 1).start()
    two_real = jnp.concatenate([row_real, row_real * theta], axis=0)
    two_imag = jnp.concatenate([row_imag, row_imag * theta], axis=0)
    two_real, two_imag = step(last, two_real, two_imag, product_rows)
    two_real = jnp.concatenate([two_real[:mon] * theta, two_real], axis=0)
    two_imag = jnp.concatenate([two_imag[:mon] * theta, two_imag], axis=0)
    operands = [
        jnp.concatenate([tail[k], x], axis=0) for k, x in enumerate(lefts(two_real, two_imag))
    ]
    real, imag = multiply(operands, rights(real, imag))
    kept[1, 0], kept[1, 1] = real[:harm], imag[:harm]
    out(1, 0).start()
    out(1, 1).start()
    at = tail.shape[1]
    strength = scale[...]
    seen_real, seen_imag = real[at + mon : at + 2 * mon] * strength, imag[at + mon : at + 2 * mon] * strength
    totals = [
        jnp.sum(
            seen_real * imag[top : top + mon] - seen_imag * real[top : top + mon],
            axis=(0, 1), keepdims=True,
        )
        for top in (at, at + 2 * mon)
    ]
    slopes[...] = -2.0 * jnp.concatenate(totals, axis=1)
    slope_copy = pltpu.make_async_copy(slopes, gradient, slope_sem)
    slope_copy.start()
    for j in range(2):
        out(j, 0).wait()
        out(j, 1).wait()
    slope_copy.wait()


def local(pattern, thickness, coupling, angles, points, incident, monitors, weights):
    sections = lax.axis_size("sect")
    own_layers = pattern.shape[0]
    assert own_layers == 2
    patterns, harm = coupling.shape[0], incident.shape[-1]
    layers = sections * own_layers
    depth = depth_of(harm)
    vmem = pl.BlockSpec(memory_space=pltpu.VMEM)
    hbm = pl.BlockSpec(memory_space=pltpu.HBM)
    mon = monitors.shape[0]
    *tables, prepared, start = pl.pallas_call(
        functools.partial(gather_kernel, sections),
        out_shape=(
            jax.ShapeDtypeStruct((sections, 1, LANES), f32),
            jax.ShapeDtypeStruct((sections, 1, LANES), jnp.int32),
            jax.ShapeDtypeStruct((1, harm), f32),
            jax.ShapeDtypeStruct((mon, harm), f32),
            jax.ShapeDtypeStruct((mon, harm), f32),
            jax.ShapeDtypeStruct((2, harm, harm), f32),
            jax.ShapeDtypeStruct((3, harm + -harm % 16, depth), bf16),
            jax.ShapeDtypeStruct((patterns, 3, depth, harm), bf16),
            jax.ShapeDtypeStruct((3, depth, harm), bf16),
        ),
        in_specs=[hbm] * 7 + [pl.BlockSpec(memory_space=pl.ANY)],
        out_specs=(vmem,) * 9,
        scratch_shapes=[
            pltpu.SMEM((own_layers,), jnp.int32),
            pltpu.SMEM((own_layers,), f32),
            pltpu.VMEM(angles.shape, f32),
            pltpu.SMEM((mon,), jnp.int32),
            pltpu.SMEM((mon,), f32),
            pltpu.VMEM((1, 1), jnp.int32),
            pltpu.VMEM((1, LANES), f32),
            pltpu.VMEM((2, harm, harm), f32),
            pltpu.VMEM((patterns, 2, harm, harm), f32),
            pltpu.SemaphoreType.DMA((6,)),
            pltpu.SemaphoreType.DMA((sections,)),
            pltpu.SemaphoreType.DMA((sections,)),
            pltpu.SemaphoreType.DMA((patterns, 2)),
            pltpu.SemaphoreType.DMA((2,)),
        ],
        compiler_params=pltpu.CompilerParams(
            collective_id=0, has_side_effects=True, vmem_limit_bytes=14 * 2**20
        ),
    )(
        *(
            pltpu.with_memory_space_constraint(x, pltpu.HBM)
            for x in (
                pattern, thickness, angles, monitors, weights,
                coupling.transpose(0, 2, 1, 3), incident.transpose(0, 2, 1, 3),
            )
        ),
        points[None],
    )
    gathered, index, theta, picked, scale, head, tail = tables
    fields, gradient = pl.pallas_call(
        functools.partial(main_kernel, own_layers),
        out_shape=(
            jax.ShapeDtypeStruct((own_layers, 1, harm, 2, harm), f32),
            jax.ShapeDtypeStruct((1, own_layers), f32),
        ),
        in_specs=[vmem] * 9,
        out_specs=(hbm, hbm),
        scratch_shapes=[
            pltpu.SMEM((layers,), jnp.int32),
            pltpu.VMEM((own_layers, sections, harm), f32),
            pltpu.VMEM((own_layers, sections, harm), f32),
            pltpu.VMEM((2, 2, harm, harm), f32),
            pltpu.VMEM((1, own_layers), f32),
            pltpu.VMEM((2, mon, harm), f32),
            pltpu.VMEM((4, harm, harm), f32),
            pltpu.VMEM((4, harm, harm), f32),
            pltpu.SemaphoreType.DMA,
            pltpu.SemaphoreType.DMA((2, 2)),
        ],
        compiler_params=pltpu.CompilerParams(vmem_limit_bytes=16 * 2**20),
    )(index, gathered, theta, picked, scale, head, tail, prepared, start)
    return fields.transpose(0, 1, 3, 2, 4), gradient


def solution(mesh):
    in_specs = (
        P("sect"), P("sect"), P(), P(), P("groups"),
        P("groups", None, None, None), P(), P(),
    )
    out_specs = (P("sect", "groups", None, None, None), P("groups", "sect"))
    return jax.shard_map(local, mesh=mesh, in_specs=in_specs, out_specs=out_specs, check_vma=False)
```

```python
import functools
import math
import jax
import jax.numpy as jnp
from jax import lax
from jax.experimental import pallas as pl
from jax.experimental.pallas import tpu as pltpu
from jax.sharding import PartitionSpec as P

norm_scale = (1.0 + 1.0 / 22.0) ** (-0.5)
f32 = jnp.float32
bf16 = jnp.bfloat16
LANES = 128
UNROLL = (5, 2, 1)


def cut_of(harm):
    cut = harm // LANES * LANES
    rest = harm - cut
    assert 3 * rest <= LANES
    return cut, rest


def split(x):
    hi = x.astype(bf16)
    return hi, (x - hi.astype(f32)).astype(bf16)


def depth_of(harm):
    return 3 * cut_of(harm)[0] + LANES


def left(x):
    cut, rest = cut_of(x.shape[1])
    hi, lo = split(x)
    a, b = hi[:, cut:], lo[:, cut:]
    zero = jnp.zeros((x.shape[0], LANES - 3 * rest), bf16)
    return jnp.concatenate([hi[:, :cut], lo[:, :cut], hi[:, :cut], a, b, a, zero], axis=1)


def right_parts(x):
    cut, rest = cut_of(x.shape[0])
    hi = x.astype(bf16)
    wide = hi.astype(f32)
    lo = x - wide
    zero = jnp.zeros((LANES - 3 * rest, x.shape[1]), f32)
    tail = jnp.concatenate([wide[cut:], wide[cut:], lo[cut:], zero], axis=0)
    return hi[:cut], lo[:cut].astype(bf16), tail.astype(bf16)


def right(x):
    hi, lo, tail = right_parts(x)
    return jnp.concatenate([hi, hi, lo, tail], axis=0)


def rights(real, imag):
    return [right(real), right(imag - real), right(real + imag)]


def dot(a, b):
    return lax.dot_general(a, b, (((1,), (0,)), ((), ())), preferred_element_type=f32)


def lefts(real, imag):
    return left(real + imag), left(real), left(imag)


def multiply(operands, weights):
    both, first, second = (dot(x, y) for x, y in zip(operands, weights))
    return both - second, both + first


def product(real, imag, weights):
    return multiply(lefts(real, imag), weights)


def product_rows(real, imag, weights):
    m = real.shape[0]
    both = left(jnp.concatenate([real + imag, real - imag], axis=0))
    low, high = dot(both, weights[1]), dot(both, weights[2])
    return 0.5 * (high[m:] - low[:m]), 0.5 * (high[:m] + low[m:])


def turns_of(x):
    k = jnp.floor(x * (2.0 / math.pi) + 0.5)
    r = ((x - k * 1.5703125) - k * 4.837512969970703e-4) - k * 7.549789948768648e-8
    z = r * r
    sin = r + r * z * (-1.6666654611e-1 + z * (8.3321608736e-3 + z * -1.9515295891e-4))
    cos = 1.0 - 0.5 * z + z * z * (
        4.166664568298827e-2 + z * (-1.388731625493765e-3 + z * 2.443315711809948e-5)
    )
    q = k.astype(jnp.int32) & 3
    odd = (q & 1) == 1
    cos, sin = jnp.where(odd, sin, cos), jnp.where(odd, cos, sin)
    cos = jnp.where((q == 1) | (q == 2), -cos, cos)
    sin = jnp.where(q >= 2, -sin, sin)
    return norm_scale * cos, norm_scale * sin


def store_right(ref, at, x):
    hi, lo, tail = right_parts(x)
    cut = hi.shape[0]
    ref[at + (pl.ds(0, cut),)] = hi
    ref[at + (pl.ds(cut, cut),)] = hi
    ref[at + (pl.ds(2 * cut, cut),)] = lo
    ref[at + (pl.ds(3 * cut, LANES),)] = tail


def each(low, high, act):
    if high - low <= 16:
        for k in range(low, high):
            act(k)
    else:
        lax.fori_loop(low, high, lambda k, c: (act(k), c)[1], 0)


def gather_kernel(
    count, pattern, thickness, angles, monitors, strengths, coupling, incident, points,
    out_ref, index_ref, theta_ref, picked_ref, scale_ref, head, tail, weights, start,
    own_pattern, own_thickness, own_angles, own_monitors, own_strengths, own_point, own_ref, waves, mixing,
    own_sem, send_sem, recv_sem, load_sem, wave_sem,
):
    here = lax.axis_index("sect")
    barrier = pltpu.get_barrier_semaphore()
    patterns = coupling.shape[0]
    harm = coupling.shape[-1]
    own_layers = pattern.shape[0]
    mesh_id = pl.DeviceIdType.MESH

    def peer(k):
        return lax.rem(here + k, count)

    def greet(k):
        pl.semaphore_signal(barrier, inc=1, device_id={"sect": peer(k)}, device_id_type=mesh_id)

    own_copies = [
        pltpu.make_async_copy(source, target, own_sem.at[k])
        for k, (source, target) in enumerate((
            (pattern, own_pattern), (thickness, own_thickness), (angles, own_angles),
            (monitors, own_monitors), (strengths, own_strengths), (points, own_point),
        ))
    ]
    for copy in own_copies:
        copy.start()
    each(1, count, greet)

    bunch = 4 if patterns % 4 == 0 else 1
    bunches = patterns // bunch

    def load(b, r):
        some = pl.ds(b * bunch, bunch)
        return pltpu.make_async_copy(coupling.at[some, :, r, :], mixing.at[some, r], load_sem.at[b, r])

    def load_start(b, c):
        load(b, 0).start()
        load(b, 1).start()
        return c

    lax.fori_loop(0, bunches, load_start, 0)
    wave = [
        pltpu.make_async_copy(incident.at[0, :, r, :], waves.at[r], wave_sem.at[r]) for r in range(2)
    ]
    for copy in wave:
        copy.start()

    for copy in own_copies[:2]:
        copy.wait()
    lanes = lax.broadcasted_iota(jnp.int32, (1, LANES), 1)
    own = jnp.zeros((1, LANES), f32)
    for j in range(own_layers):
        own = jnp.where(lanes == j, own_pattern[j].astype(f32), own)
        own = jnp.where(lanes == own_layers + j, own_thickness[j], own)
    own_ref[...] = own
    out_ref[here] = own
    rows = lax.broadcasted_iota(jnp.int32, (harm, harm), 0)
    columns = lax.broadcasted_iota(jnp.int32, (harm, harm), 1)
    unit = jnp.where(rows == columns, 1.0, 0.0).astype(f32)

    def prepare_one(n, c):
        real, imag = unit + mixing[n, 0], mixing[n, 1]
        store_right(weights, (n, 0), real)
        store_right(weights, (n, 1), imag - real)
        store_right(weights, (n, 2), real + imag)
        return c

    def prepare(b, c):
        load(b, 0).wait()
        load(b, 1).wait()
        return lax.fori_loop(b * bunch, (b + 1) * bunch, prepare_one, c)

    early = jnp.where(here < 2, 3 * bunches // 4, jnp.where(here < count // 2, bunches // 4, 0))
    lax.fori_loop(0, early, prepare, 0)
    pl.semaphore_wait(barrier, count - 1)

    def send(k):
        return pltpu.make_async_remote_copy(
            src_ref=own_ref,
            dst_ref=out_ref.at[here],
            send_sem=send_sem.at[k],
            recv_sem=recv_sem.at[k],
            device_id={"sect": peer(k)},
            device_id_type=mesh_id,
        )

    each(1, count, lambda k: send(k).start())

    for copy in own_copies[2:]:
        copy.wait()
    entries = lax.broadcasted_iota(jnp.int32, own_angles.shape, 0)
    theta = jnp.sum(jnp.where(entries == own_point[...], own_angles[...], 0.0), axis=0, keepdims=True)
    theta_ref[...] = theta
    mon = monitors.shape[0]
    pick_rows = lax.broadcasted_iota(jnp.int32, (mon, harm), 0)
    pick_lanes = lax.broadcasted_iota(jnp.int32, (mon, harm), 1)
    picked = jnp.zeros((mon, harm), f32)
    scale = jnp.zeros((mon, harm), f32)
    for m in range(mon):
        picked = jnp.where((pick_rows == m) & (pick_lanes == own_monitors[m]), 1.0, picked)
        scale = jnp.where(pick_rows == m, own_strengths[m], scale)
    picked_ref[...] = picked
    scale_ref[...] = scale * (1.0 / harm)
    turns = jnp.concatenate([theta * own_thickness[j] for j in range(own_layers)], axis=0)
    turns = jnp.concatenate([*turns_of(turns), jnp.zeros((8 - 2 * own_layers, harm), f32)], axis=0).T

    lax.fori_loop(early, bunches, prepare, 0)
    for copy in wave:
        copy.wait()
    real, imag = waves[0], waves[1]
    store_right(start, (0,), real)
    store_right(start, (1,), imag - real)
    store_right(start, (2,), real + imag)

    def transfer(j):
        cos, sin = turns[:, j : j + 1], turns[:, own_layers + j : own_layers + j + 1]
        n = own_pattern[j]
        real, imag = unit + mixing[n, 0], mixing[n, 1]
        return cos * real - sin * imag, cos * imag + sin * real

    head[0], head[1] = transfer(0)
    gap = jnp.zeros((-harm % 16, harm), f32)
    real, imag = (jnp.concatenate([x, gap], axis=0) for x in transfer(1))
    for k, x in enumerate(lefts(real, imag)):
        tail[k] = x
    each(1, count, lambda k: send(k).wait())
    index_ref[...] = out_ref[...].astype(jnp.int32)


def main_kernel(
    own_layers, index_ref, gathered, theta_ref, picked, scale, head, tail, weights, start,
    fields, gradient, index, cosines, sines, kept, slopes, row_state, sub_state, pair_state, slope_sem, out_sem,
):
    here = lax.axis_index("sect")
    sections = gathered.shape[0]
    layers = sections * own_layers
    mon, harm = picked.shape
    first = here * own_layers
    last = first + 1
    theta = theta_ref[...]

    depths = gathered[:, 0, :]
    for t in range(own_layers):
        turn = depths[:, own_layers + t : own_layers + t + 1] * theta
        cosines[t], sines[t] = turns_of(turn)

    def note(j, c):
        row = index_ref[j]
        for t in range(own_layers):
            index[j * own_layers + t] = row[0, t]
        return c

    lax.fori_loop(0, sections, note, 0, unroll=16)

    def step(layer, real, imag, form=product):
        section, t = layer // own_layers, lax.rem(layer, own_layers)
        cos, sin = cosines[t, pl.ds(section, 1), :], sines[t, pl.ds(section, 1), :]
        n = index[layer]
        return form(
            cos * real - sin * imag, cos * imag + sin * real,
            (weights[n, 0], weights[n, 1], weights[n, 2]),
        )

    def move(state, layer, form):
        state[0], state[1] = step(layer, state[0], state[1], form)

    def loop(count, body):
        done = 0
        for size in UNROLL:
            def several(i, c, size=size, done=done):
                for j in range(size):
                    body(done + size * i + j)
                return c

            times = (count - done) // size
            lax.fori_loop(0, times, several, 0)
            done = done + times * size

    rows = lax.broadcasted_iota(jnp.int32, (harm, harm), 0)
    columns = lax.broadcasted_iota(jnp.int32, (harm, harm), 1)
    unit = jnp.where(rows == columns, 1.0, 0.0).astype(f32)
    none = jnp.zeros((harm, harm), f32)
    top, low = pair_state.at[pl.ds(0, 2)], pair_state.at[pl.ds(2, 2)]

    row_state[0], row_state[1] = picked[...], jnp.zeros((mon, harm), f32)
    upper, under = sub_state.at[pl.ds(0, 2)], sub_state.at[pl.ds(2, 2)]
    upper[0], upper[1] = unit, none
    under[0], under[1] = unit, none
    top[0], top[1] = head[0], head[1]
    low[0], low[1] = unit, none
    behind = layers - first - own_layers
    third = behind // 3
    high = layers - 1 - (behind - 2 * third)

    def suffix(k):
        move(upper, high - k, product)
        move(under, high - third - k, product)
        move(row_state, layers - 1 - k, product_rows)

    def suffix_rest(k, c):
        move(row_state, layers - 1 - third - k, product_rows)
        return c

    loop(third, suffix)
    lax.fori_loop(0, behind - 3 * third, suffix_rest, 0)

    def prefix(k):
        move(top, first - 1 - k, product)
        move(low, first // 2 - 1 - k, product)

    loop(first // 2, prefix)

    real, imag = product(low[0], low[1], (start[0], start[1], start[2]))
    row_real, row_imag = product_rows(row_state[0], row_state[1], rights(upper[0], upper[1]))
    real, imag = product(top[0], top[1], rights(real, imag))
    row_real, row_imag = product_rows(row_real, row_imag, rights(under[0], under[1]))
    kept[0, 0], kept[0, 1] = real, imag

    def out(j, r):
        return pltpu.make_async_copy(kept.at[j, r], fields.at[j, 0, :, r, :], out_sem.at[j, r])

    out(0, 0).start()
    out(0, 1).start()
    two_real = jnp.concatenate([row_real, row_real * theta], axis=0)
    two_imag = jnp.concatenate([row_imag, row_imag * theta], axis=0)
    two_real, two_imag = step(last, two_real, two_imag, product_rows)
    two_real = jnp.concatenate([two_real[:mon] * theta, two_real], axis=0)
    two_imag = jnp.concatenate([two_imag[:mon] * theta, two_imag], axis=0)
    operands = [
        jnp.concatenate([tail[k], x], axis=0) for k, x in enumerate(lefts(two_real, two_imag))
    ]
    real, imag = multiply(operands, rights(real, imag))
    kept[1, 0], kept[1, 1] = real[:harm], imag[:harm]
    out(1, 0).start()
    out(1, 1).start()
    at = tail.shape[1]
    strength = scale[...]
    seen_real, seen_imag = real[at + mon : at + 2 * mon] * strength, imag[at + mon : at + 2 * mon] * strength
    totals = [
        jnp.sum(
            seen_real * imag[top : top + mon] - seen_imag * real[top : top + mon],
            axis=(0, 1), keepdims=True,
        )
        for top in (at, at + 2 * mon)
    ]
    slopes[...] = -2.0 * jnp.concatenate(totals, axis=1)
    slope_copy = pltpu.make_async_copy(slopes, gradient, slope_sem)
    slope_copy.start()
    for j in range(2):
        out(j, 0).wait()
        out(j, 1).wait()
    slope_copy.wait()


def local(pattern, thickness, coupling, angles, points, incident, monitors, weights):
    sections = lax.axis_size("sect")
    own_layers = pattern.shape[0]
    assert own_layers == 2
    patterns, harm = coupling.shape[0], incident.shape[-1]
    layers = sections * own_layers
    depth = depth_of(harm)
    vmem = pl.BlockSpec(memory_space=pltpu.VMEM)
    hbm = pl.BlockSpec(memory_space=pltpu.HBM)
    mon = monitors.shape[0]
    *tables, prepared, start = pl.pallas_call(
        functools.partial(gather_kernel, sections),
        out_shape=(
            jax.ShapeDtypeStruct((sections, 1, LANES), f32),
            jax.ShapeDtypeStruct((sections, 1, LANES), jnp.int32),
            jax.ShapeDtypeStruct((1, harm), f32),
            jax.ShapeDtypeStruct((mon, harm), f32),
            jax.ShapeDtypeStruct((mon, harm), f32),
            jax.ShapeDtypeStruct((2, harm, harm), f32),
            jax.ShapeDtypeStruct((3, harm + -harm % 16, depth), bf16),
            jax.ShapeDtypeStruct((patterns, 3, depth, harm), bf16),
            jax.ShapeDtypeStruct((3, depth, harm), bf16),
        ),
        in_specs=[hbm] * 7 + [pl.BlockSpec(memory_space=pl.ANY)],
        out_specs=(vmem,) * 9,
        scratch_shapes=[
            pltpu.SMEM((own_layers,), jnp.int32),
            pltpu.SMEM((own_layers,), f32),
            pltpu.VMEM(angles.shape, f32),
            pltpu.SMEM((mon,), jnp.int32),
            pltpu.SMEM((mon,), f32),
            pltpu.VMEM((1, 1), jnp.int32),
            pltpu.VMEM((1, LANES), f32),
            pltpu.VMEM((2, harm, harm), f32),
            pltpu.VMEM((patterns, 2, harm, harm), f32),
            pltpu.SemaphoreType.DMA((6,)),
            pltpu.SemaphoreType.DMA((sections,)),
            pltpu.SemaphoreType.DMA((sections,)),
            pltpu.SemaphoreType.DMA((patterns, 2)),
            pltpu.SemaphoreType.DMA((2,)),
        ],
        compiler_params=pltpu.CompilerParams(
            collective_id=0, has_side_effects=True, vmem_limit_bytes=14 * 2**20
        ),
    )(
        *(
            pltpu.with_memory_space_constraint(x, pltpu.HBM)
            for x in (
                pattern, thickness, angles, monitors, weights,
                coupling.transpose(0, 2, 1, 3), incident.transpose(0, 2, 1, 3),
            )
        ),
        points[None],
    )
    gathered, index, theta, picked, scale, head, tail = tables
    fields, gradient = pl.pallas_call(
        functools.partial(main_kernel, own_layers),
        out_shape=(
            jax.ShapeDtypeStruct((own_layers, 1, harm, 2, harm), f32),
            jax.ShapeDtypeStruct((1, own_layers), f32),
        ),
        in_specs=[vmem] * 9,
        out_specs=(hbm, hbm),
        scratch_shapes=[
            pltpu.SMEM((layers,), jnp.int32),
            pltpu.VMEM((own_layers, sections, harm), f32),
            pltpu.VMEM((own_layers, sections, harm), f32),
            pltpu.VMEM((2, 2, harm, harm), f32),
            pltpu.VMEM((1, own_layers), f32),
            pltpu.VMEM((2, mon, harm), f32),
            pltpu.VMEM((4, harm, harm), f32),
            pltpu.VMEM((4, harm, harm), f32),
            pltpu.SemaphoreType.DMA,
            pltpu.SemaphoreType.DMA((2, 2)),
        ],
        compiler_params=pltpu.CompilerParams(vmem_limit_bytes=16 * 2**20),
    )(index, gathered, theta, picked, scale, head, tail, prepared, start)
    return fields.transpose(0, 1, 3, 2, 4), gradient


def solution(mesh):
    in_specs = (
        P("sect"), P("sect"), P(), P(), P("groups"),
        P("groups", None, None, None), P(), P(),
    )
    out_specs = (P("sect", "groups", None, None, None), P("groups", "sect"))
    return jax.shard_map(local, mesh=mesh, in_specs=in_specs, out_specs=out_specs, check_vma=False)
```

```python
import functools
import math
import jax
import jax.numpy as jnp
from jax import lax
from jax.experimental import pallas as pl
from jax.experimental.pallas import tpu as pltpu
from jax.sharding import PartitionSpec as P

norm_scale = (1.0 + 1.0 / 22.0) ** (-0.5)
f32 = jnp.float32
bf16 = jnp.bfloat16
LANES = 128
UNROLL = (5, 2, 1)


def cut_of(harm):
    cut = harm // LANES * LANES
    rest = harm - cut
    assert 3 * rest <= LANES
    return cut, rest


def split(x):
    hi = x.astype(bf16)
    return hi, (x - hi.astype(f32)).astype(bf16)


def depth_of(harm):
    return 3 * cut_of(harm)[0] + LANES


def left(x):
    cut, rest = cut_of(x.shape[1])
    hi, lo = split(x)
    a, b = hi[:, cut:], lo[:, cut:]
    zero = jnp.zeros((x.shape[0], LANES - 3 * rest), bf16)
    return jnp.concatenate([hi[:, :cut], lo[:, :cut], hi[:, :cut], a, b, a, zero], axis=1)


def right_parts(x):
    cut, rest = cut_of(x.shape[0])
    hi = x.astype(bf16)
    wide = hi.astype(f32)
    lo = x - wide
    zero = jnp.zeros((LANES - 3 * rest, x.shape[1]), f32)
    tail = jnp.concatenate([wide[cut:], wide[cut:], lo[cut:], zero], axis=0)
    return hi[:cut], lo[:cut].astype(bf16), tail.astype(bf16)


def right(x):
    hi, lo, tail = right_parts(x)
    return jnp.concatenate([hi, hi, lo, tail], axis=0)


def rights(real, imag):
    return [right(real), right(imag - real), right(real + imag)]


def dot(a, b):
    return lax.dot_general(a, b, (((1,), (0,)), ((), ())), preferred_element_type=f32)


def lefts(real, imag):
    return left(real + imag), left(real), left(imag)


def multiply(operands, weights):
    both, first, second = (dot(x, y) for x, y in zip(operands, weights))
    return both - second, both + first


def product(real, imag, weights):
    return multiply(lefts(real, imag), weights)


def product_rows(real, imag, weights):
    m = real.shape[0]
    both = left(jnp.concatenate([real + imag, real - imag], axis=0))
    low, high = dot(both, weights[1]), dot(both, weights[2])
    return 0.5 * (high[m:] - low[:m]), 0.5 * (high[:m] + low[m:])


def turns_of(x):
    k = jnp.floor(x * (2.0 / math.pi) + 0.5)
    r = ((x - k * 1.5703125) - k * 4.837512969970703e-4) - k * 7.549789948768648e-8
    z = r * r
    sin = r + r * z * (-1.6666654611e-1 + z * (8.3321608736e-3 + z * -1.9515295891e-4))
    cos = 1.0 - 0.5 * z + z * z * (
        4.166664568298827e-2 + z * (-1.388731625493765e-3 + z * 2.443315711809948e-5)
    )
    q = k.astype(jnp.int32) & 3
    odd = (q & 1) == 1
    cos, sin = jnp.where(odd, sin, cos), jnp.where(odd, cos, sin)
    cos = jnp.where((q == 1) | (q == 2), -cos, cos)
    sin = jnp.where(q >= 2, -sin, sin)
    return norm_scale * cos, norm_scale * sin


def store_right(ref, at, x):
    hi, lo, tail = right_parts(x)
    cut = hi.shape[0]
    ref[at + (pl.ds(0, cut),)] = hi
    ref[at + (pl.ds(cut, cut),)] = hi
    ref[at + (pl.ds(2 * cut, cut),)] = lo
    ref[at + (pl.ds(3 * cut, LANES),)] = tail


def each(low, high, act):
    if high - low <= 16:
        for k in range(low, high):
            act(k)
    else:
        lax.fori_loop(low, high, lambda k, c: (act(k), c)[1], 0)


def gather_kernel(
    count, pattern, thickness, angles, monitors, strengths, coupling, incident, points,
    out_ref, index_ref, theta_ref, picked_ref, scale_ref, head, tail, weights, start,
    own_pattern, own_thickness, own_angles, own_monitors, own_strengths, own_point, own_ref, waves, mixing,
    own_sem, send_sem, recv_sem, load_sem, wave_sem,
):
    here = lax.axis_index("sect")
    barrier = pltpu.get_barrier_semaphore()
    patterns = coupling.shape[0]
    harm = coupling.shape[-1]
    own_layers = pattern.shape[0]
    mesh_id = pl.DeviceIdType.MESH

    def peer(k):
        return lax.rem(here + k, count)

    def greet(k):
        pl.semaphore_signal(barrier, inc=1, device_id={"sect": peer(k)}, device_id_type=mesh_id)

    own_copies = [
        pltpu.make_async_copy(source, target, own_sem.at[k])
        for k, (source, target) in enumerate((
            (pattern, own_pattern), (thickness, own_thickness), (angles, own_angles),
            (monitors, own_monitors), (strengths, own_strengths), (points, own_point),
        ))
    ]
    for copy in own_copies:
        copy.start()
    each(1, count, greet)

    bunch = 4 if patterns % 4 == 0 else 1
    bunches = patterns // bunch

    def load(b, r):
        some = pl.ds(b * bunch, bunch)
        return pltpu.make_async_copy(coupling.at[some, :, r, :], mixing.at[some, r], load_sem.at[b, r])

    def load_start(b, c):
        load(b, 0).start()
        load(b, 1).start()
        return c

    lax.fori_loop(0, bunches, load_start, 0)
    wave = [
        pltpu.make_async_copy(incident.at[0, :, r, :], waves.at[r], wave_sem.at[r]) for r in range(2)
    ]
    for copy in wave:
        copy.start()

    for copy in own_copies[:2]:
        copy.wait()
    lanes = lax.broadcasted_iota(jnp.int32, (1, LANES), 1)
    own = jnp.zeros((1, LANES), f32)
    for j in range(own_layers):
        own = jnp.where(lanes == j, own_pattern[j].astype(f32), own)
        own = jnp.where(lanes == own_layers + j, own_thickness[j], own)
    own_ref[...] = own
    out_ref[here] = own
    rows = lax.broadcasted_iota(jnp.int32, (harm, harm), 0)
    columns = lax.broadcasted_iota(jnp.int32, (harm, harm), 1)
    unit = jnp.where(rows == columns, 1.0, 0.0).astype(f32)

    def prepare_one(n, c):
        real, imag = unit + mixing[n, 0], mixing[n, 1]
        store_right(weights, (n, 0), real)
        store_right(weights, (n, 1), imag - real)
        store_right(weights, (n, 2), real + imag)
        return c

    def prepare(b, c):
        load(b, 0).wait()
        load(b, 1).wait()
        return lax.fori_loop(b * bunch, (b + 1) * bunch, prepare_one, c)

    early = jnp.where(here < 2, 3 * bunches // 4, jnp.where(here < count // 2, bunches // 4, 0))
    lax.fori_loop(0, early, prepare, 0)
    pl.semaphore_wait(barrier, count - 1)

    def send(k):
        return pltpu.make_async_remote_copy(
            src_ref=own_ref,
            dst_ref=out_ref.at[here],
            send_sem=send_sem.at[k],
            recv_sem=recv_sem.at[k],
            device_id={"sect": peer(k)},
            device_id_type=mesh_id,
        )

    each(1, count, lambda k: send(k).start())

    for copy in own_copies[2:]:
        copy.wait()
    entries = lax.broadcasted_iota(jnp.int32, own_angles.shape, 0)
    theta = jnp.sum(jnp.where(entries == own_point[...], own_angles[...], 0.0), axis=0, keepdims=True)
    theta_ref[...] = theta
    mon = monitors.shape[0]
    pick_rows = lax.broadcasted_iota(jnp.int32, (mon, harm), 0)
    pick_lanes = lax.broadcasted_iota(jnp.int32, (mon, harm), 1)
    picked = jnp.zeros((mon, harm), f32)
    scale = jnp.zeros((mon, harm), f32)
    for m in range(mon):
        picked = jnp.where((pick_rows == m) & (pick_lanes == own_monitors[m]), 1.0, picked)
        scale = jnp.where(pick_rows == m, own_strengths[m], scale)
    picked_ref[...] = picked
    scale_ref[...] = scale * (1.0 / harm)
    turns = jnp.concatenate([theta * own_thickness[j] for j in range(own_layers)], axis=0)
    turns = jnp.concatenate([*turns_of(turns), jnp.zeros((8 - 2 * own_layers, harm), f32)], axis=0).T

    lax.fori_loop(early, bunches, prepare, 0)
    for copy in wave:
        copy.wait()
    real, imag = waves[0], waves[1]
    store_right(start, (0,), real)
    store_right(start, (1,), imag - real)
    store_right(start, (2,), real + imag)

    def transfer(j):
        cos, sin = turns[:, j : j + 1], turns[:, own_layers + j : own_layers + j + 1]
        n = own_pattern[j]
        real, imag = unit + mixing[n, 0], mixing[n, 1]
        return cos * real - sin * imag, cos * imag + sin * real

    head[0], head[1] = transfer(0)
    gap = jnp.zeros((-harm % 16, harm), f32)
    real, imag = (jnp.concatenate([x, gap], axis=0) for x in transfer(1))
    for k, x in enumerate(lefts(real, imag)):
        tail[k] = x
    each(1, count, lambda k: send(k).wait())
    index_ref[...] = out_ref[...].astype(jnp.int32)


def main_kernel(
    own_layers, index_ref, gathered, theta_ref, picked, scale, head, tail, weights, start,
    fields, gradient, index, cosines, sines, kept, slopes, row_state, sub_state, pair_state, slope_sem, out_sem,
):
    here = lax.axis_index("sect")
    sections = gathered.shape[0]
    layers = sections * own_layers
    mon, harm = picked.shape
    first = here * own_layers
    last = first + 1
    theta = theta_ref[...]

    depths = gathered[:, 0, :]
    for t in range(own_layers):
        turn = depths[:, own_layers + t : own_layers + t + 1] * theta
        cosines[t], sines[t] = turns_of(turn)

    def note(j, c):
        row = index_ref[j]
        for t in range(own_layers):
            index[j * own_layers + t] = row[0, t]
        return c

    lax.fori_loop(0, sections, note, 0, unroll=16)

    def step(layer, real, imag, form=product):
        section, t = layer // own_layers, lax.rem(layer, own_layers)
        cos, sin = cosines[t, pl.ds(section, 1), :], sines[t, pl.ds(section, 1), :]
        n = index[layer]
        return form(
            cos * real - sin * imag, cos * imag + sin * real,
            (weights[n, 0], weights[n, 1], weights[n, 2]),
        )

    def move(state, layer, form):
        state[0], state[1] = step(layer, state[0], state[1], form)

    def turned(state, layer):
        section, t = layer // own_layers, lax.rem(layer, own_layers)
        cos, sin = cosines[t, pl.ds(section, 1), :], sines[t, pl.ds(section, 1), :]
        real, imag = state[0], state[1]
        return cos * real - sin * imag, cos * imag + sin * real

    def move_two(state_a, one, state_b, two):
        n, m = index[one], index[two]
        a = lefts(*turned(state_a, one))
        real, imag = turned(state_b, two)
        a_both, b0 = dot(a[0], weights[n, 0]), left(real + imag)
        a_first, b1 = dot(a[1], weights[n, 1]), left(real)
        a_second, b2 = dot(a[2], weights[n, 2]), left(imag)
        b_both = dot(b0, weights[m, 0])
        state_a[0], state_a[1] = a_both - a_second, a_both + a_first
        b_first, b_second = dot(b1, weights[m, 1]), dot(b2, weights[m, 2])
        state_b[0], state_b[1] = b_both - b_second, b_both + b_first

    def loop(count, body):
        done = 0
        for size in UNROLL:
            def several(i, c, size=size, done=done):
                for j in range(size):
                    body(done + size * i + j)
                return c

            times = (count - done) // size
            lax.fori_loop(0, times, several, 0)
            done = done + times * size

    rows = lax.broadcasted_iota(jnp.int32, (harm, harm), 0)
    columns = lax.broadcasted_iota(jnp.int32, (harm, harm), 1)
    unit = jnp.where(rows == columns, 1.0, 0.0).astype(f32)
    none = jnp.zeros((harm, harm), f32)
    top, low = pair_state.at[pl.ds(0, 2)], pair_state.at[pl.ds(2, 2)]

    row_state[0], row_state[1] = picked[...], jnp.zeros((mon, harm), f32)
    upper, under = sub_state.at[pl.ds(0, 2)], sub_state.at[pl.ds(2, 2)]
    upper[0], upper[1] = unit, none
    under[0], under[1] = unit, none
    top[0], top[1] = head[0], head[1]
    low[0], low[1] = unit, none
    behind = layers - first - own_layers
    third = behind // 3
    high = layers - 1 - (behind - 2 * third)

    def suffix(k):
        move_two(upper, high - k, under, high - third - k)
        move(row_state, layers - 1 - k, product_rows)

    def suffix_rest(k, c):
        move(row_state, layers - 1 - third - k, product_rows)
        return c

    loop(third, suffix)
    lax.fori_loop(0, behind - 3 * third, suffix_rest, 0)

    def prefix(k):
        move_two(top, first - 1 - k, low, first // 2 - 1 - k)

    loop(first // 2, prefix)

    real, imag = product(low[0], low[1], (start[0], start[1], start[2]))
    row_real, row_imag = product_rows(row_state[0], row_state[1], rights(upper[0], upper[1]))
    real, imag = product(top[0], top[1], rights(real, imag))
    row_real, row_imag = product_rows(row_real, row_imag, rights(under[0], under[1]))
    kept[0, 0], kept[0, 1] = real, imag

    def out(j, r):
        return pltpu.make_async_copy(kept.at[j, r], fields.at[j, 0, :, r, :], out_sem.at[j, r])

    out(0, 0).start()
    out(0, 1).start()
    two_real = jnp.concatenate([row_real, row_real * theta], axis=0)
    two_imag = jnp.concatenate([row_imag, row_imag * theta], axis=0)
    two_real, two_imag = step(last, two_real, two_imag, product_rows)
    two_real = jnp.concatenate([two_real[:mon] * theta, two_real], axis=0)
    two_imag = jnp.concatenate([two_imag[:mon] * theta, two_imag], axis=0)
    operands = [
        jnp.concatenate([tail[k], x], axis=0) for k, x in enumerate(lefts(two_real, two_imag))
    ]
    real, imag = multiply(operands, rights(real, imag))
    kept[1, 0], kept[1, 1] = real[:harm], imag[:harm]
    out(1, 0).start()
    out(1, 1).start()
    at = tail.shape[1]
    strength = scale[...]
    seen_real, seen_imag = real[at + mon : at + 2 * mon] * strength, imag[at + mon : at + 2 * mon] * strength
    totals = [
        jnp.sum(
            seen_real * imag[top : top + mon] - seen_imag * real[top : top + mon],
            axis=(0, 1), keepdims=True,
        )
        for top in (at, at + 2 * mon)
    ]
    slopes[...] = -2.0 * jnp.concatenate(totals, axis=1)
    slope_copy = pltpu.make_async_copy(slopes, gradient, slope_sem)
    slope_copy.start()
    for j in range(2):
        out(j, 0).wait()
        out(j, 1).wait()
    slope_copy.wait()


def local(pattern, thickness, coupling, angles, points, incident, monitors, weights):
    sections = lax.axis_size("sect")
    own_layers = pattern.shape[0]
    assert own_layers == 2
    patterns, harm = coupling.shape[0], incident.shape[-1]
    layers = sections * own_layers
    depth = depth_of(harm)
    vmem = pl.BlockSpec(memory_space=pltpu.VMEM)
    hbm = pl.BlockSpec(memory_space=pltpu.HBM)
    mon = monitors.shape[0]
    *tables, prepared, start = pl.pallas_call(
        functools.partial(gather_kernel, sections),
        out_shape=(
            jax.ShapeDtypeStruct((sections, 1, LANES), f32),
            jax.ShapeDtypeStruct((sections, 1, LANES), jnp.int32),
            jax.ShapeDtypeStruct((1, harm), f32),
            jax.ShapeDtypeStruct((mon, harm), f32),
            jax.ShapeDtypeStruct((mon, harm), f32),
            jax.ShapeDtypeStruct((2, harm, harm), f32),
            jax.ShapeDtypeStruct((3, harm + -harm % 16, depth), bf16),
            jax.ShapeDtypeStruct((patterns, 3, depth, harm), bf16),
            jax.ShapeDtypeStruct((3, depth, harm), bf16),
        ),
        in_specs=[hbm] * 7 + [pl.BlockSpec(memory_space=pl.ANY)],
        out_specs=(vmem,) * 9,
        scratch_shapes=[
            pltpu.SMEM((own_layers,), jnp.int32),
            pltpu.SMEM((own_layers,), f32),
            pltpu.VMEM(angles.shape, f32),
            pltpu.SMEM((mon,), jnp.int32),
            pltpu.SMEM((mon,), f32),
            pltpu.VMEM((1, 1), jnp.int32),
            pltpu.VMEM((1, LANES), f32),
            pltpu.VMEM((2, harm, harm), f32),
            pltpu.VMEM((patterns, 2, harm, harm), f32),
            pltpu.SemaphoreType.DMA((6,)),
            pltpu.SemaphoreType.DMA((sections,)),
            pltpu.SemaphoreType.DMA((sections,)),
            pltpu.SemaphoreType.DMA((patterns, 2)),
            pltpu.SemaphoreType.DMA((2,)),
        ],
        compiler_params=pltpu.CompilerParams(
            collective_id=0, has_side_effects=True, vmem_limit_bytes=14 * 2**20
        ),
    )(
        *(
            pltpu.with_memory_space_constraint(x, pltpu.HBM)
            for x in (
                pattern, thickness, angles, monitors, weights,
                coupling.transpose(0, 2, 1, 3), incident.transpose(0, 2, 1, 3),
            )
        ),
        points[None],
    )
    gathered, index, theta, picked, scale, head, tail = tables
    fields, gradient = pl.pallas_call(
        functools.partial(main_kernel, own_layers),
        out_shape=(
            jax.ShapeDtypeStruct((own_layers, 1, harm, 2, harm), f32),
            jax.ShapeDtypeStruct((1, own_layers), f32),
        ),
        in_specs=[vmem] * 9,
        out_specs=(hbm, hbm),
        scratch_shapes=[
            pltpu.SMEM((layers,), jnp.int32),
            pltpu.VMEM((own_layers, sections, harm), f32),
            pltpu.VMEM((own_layers, sections, harm), f32),
            pltpu.VMEM((2, 2, harm, harm), f32),
            pltpu.VMEM((1, own_layers), f32),
            pltpu.VMEM((2, mon, harm), f32),
            pltpu.VMEM((4, harm, harm), f32),
            pltpu.VMEM((4, harm, harm), f32),
            pltpu.SemaphoreType.DMA,
            pltpu.SemaphoreType.DMA((2, 2)),
        ],
        compiler_params=pltpu.CompilerParams(vmem_limit_bytes=16 * 2**20),
    )(index, gathered, theta, picked, scale, head, tail, prepared, start)
    return fields.transpose(0, 1, 3, 2, 4), gradient


def solution(mesh):
    in_specs = (
        P("sect"), P("sect"), P(), P(), P("groups"),
        P("groups", None, None, None), P(), P(),
    )
    out_specs = (P("sect", "groups", None, None, None), P("groups", "sect"))
    return jax.shard_map(local, mesh=mesh, in_specs=in_specs, out_specs=out_specs, check_vma=False)
```
